128 devices in a mesh: section: 16 (over y, x), dp: 8 (over z, core).
Axes of the slice: x: 4, y: 4, z: 4, core: 2. Of those that a mesh axis runs over, the one named last changes fastest.
Arguments:
- latents: bfloat16 [4, 1024, 320], P(None, 'dp'), may hold values from -6 to 6
- steps: int32 [8, 4], P('dp'), may hold values from 0 to 999
- cotangent: bfloat16 [4, 1024, 320], P(None, 'dp'), may hold values from -0.119628906 to 0.119628906
- w_in: bfloat16 [16, 320, 1280], P('section'), may hold values from -0.3125 to 0.3125
- w_out: bfloat16 [16, 1280, 320], P('section'), may hold values from -0.15625 to 0.15625
- w_time: bfloat16 [16, 320, 1280], P('section'), may hold values from -0.3125 to 0.3125
- w_skip: bfloat16 [16, 320, 320], P('section'), may hold values from -0.3125 to 0.3125
Outputs:
- section_out: bfloat16 [16, 4, 1024, 320], P('section', None, 'dp')
- grad_w_in: float32 [16, 320, 1280], P('section')
- grad_w_out: float32 [16, 1280, 320], P('section')
- grad_w_time: float32 [16, 320, 1280], P('section')
- grad_w_skip: float32 [16, 320, 320], P('section')
The draws below stay inside these ranges and needn't reach their ends.
All inputs are finite; a program needn't handle non-finite values.
Results may differ from the reference program's by a relative error of at most 0.03.
Values may be sent and summed in bfloat16 or wider, within the bound.
A program may use at most 64 MiB of HBM per device.

```python
import math
import jax
import jax.numpy as jnp
from jax import lax

C = 320
F = 1280
R_DEV = 128
M = 4
ROWS = 1024
N_SECTION = 16
N_DP = 8


def plant(array, stream_key, low, largest):
    extent = array.shape
    index_at = [jax.random.randint(jax.random.fold_in(stream_key, axis), (), 0, extent[axis]) for axis in range(len(extent))]
    array = array.at[tuple(index_at)].set(low)
    longest = extent.index(max(extent))
    index_at[longest] = (index_at[longest] + 1) % extent[longest]
    return array.at[tuple(index_at)].set(largest)


def block_scale(stream_key, dims, shards, low, high):
    loudness, own = 1.0, jax.random.fold_in(stream_key, 6)
    for dim, shards_of in shards:
        steps = jnp.exp(jax.random.uniform(jax.random.fold_in(own, dim), (shards_of,), jnp.float32, low / len(shards), high / len(shards)))
        loudness = loudness * jnp.repeat(steps, dims[dim] // shards_of).reshape([-1 if axis == dim else 1 for axis in range(len(dims))])
    return loudness


def scatter_about(own_key, extent, scale, bound, pieces=(), held_as=jnp.bfloat16):
    gain = block_scale(own_key, extent, pieces, -0.22, 0.18) if pieces else 1.0
    drawn = jax.random.normal(own_key, extent, jnp.float32) * scale * gain
    return jnp.minimum(jnp.maximum(drawn, -bound), bound).astype(held_as)


def setup_inputs(seed: int = 0) -> dict:
    splits = jax.random.split(jax.random.key(seed), 8)
    latents = scatter_about(splits[0], (M, ROWS, C), 1.0, 6.0, ((1, 8),))
    steps = plant(jax.random.randint(splits[1], (N_DP, M), 0, 1000), jax.random.fold_in(splits[1], 1), 0, 999).astype(jnp.int32)
    cotangent = scatter_about(splits[2], (M, ROWS, C), 0.02, 0.119628906, ((1, 8),))
    w_in = scatter_about(splits[3], (N_SECTION, C, F), C ** -0.5, 0.3125, ((0, 16),))
    w_out = scatter_about(splits[4], (N_SECTION, F, C), F ** -0.5, 0.15625, ((0, 16),))
    w_time = scatter_about(splits[5], (N_SECTION, C, F), C ** -0.5, 0.3125, ((0, 16),))
    w_skip = scatter_about(splits[6], (N_SECTION, C, C), C ** -0.5, 0.3125, ((0, 16),))
    return {"latents": latents, "steps": steps, "cotangent": cotangent, "w_in": w_in, "w_out": w_out, "w_time": w_time, "w_skip": w_skip}


def contract_rows(left, right):
    return lax.dot_general(left, right, (((0,), (0,)), ((), ())), preferred_element_type=jnp.float32)

def contract_cols(left, right):
    return lax.dot_general(left, right, (((1,), (1,)), ((), ())), preferred_element_type=jnp.float32)

def gelu_tanh(values):
    return jax.nn.gelu(values, approximate=True)

def embed(step_value, width):
    half_width = width // 2
    position = jnp.arange(half_width).astype(jnp.float32)
    frequency = jnp.exp(-math.log(10000.0) * position / half_width)
    angle = step_value.astype(jnp.float32) * frequency
    return jnp.concatenate([jnp.sin(angle), jnp.cos(angle)]).astype(jnp.bfloat16)

def inner_block(merged, w_first, w_second, w_clock, clock_code):
    widened = merged.astype(jnp.float32)
    scale = lax.rsqrt(lax.optimization_barrier(jnp.mean(widened * widened, axis=-1, keepdims=True)) + 1e-05)
    normed = (widened * scale).astype(jnp.bfloat16)
    preact = jnp.dot(normed, w_first, preferred_element_type=jnp.float32) + jnp.dot(clock_code[None, :], w_clock, preferred_element_type=jnp.float32)
    hidden = gelu_tanh(preact).astype(jnp.bfloat16)
    result = (widened + jnp.dot(hidden, w_second, preferred_element_type=jnp.float32)).astype(jnp.bfloat16)
    return (result, widened, scale, normed, preact, hidden)

def block_forward(arriving, skip_rows, w_first, w_second, w_clock, w_merge, clock_code):
    merged = (arriving.astype(jnp.float32) + jnp.dot(skip_rows, w_merge, preferred_element_type=jnp.float32)).astype(jnp.bfloat16)
    result = inner_block(merged, w_first, w_second, w_clock, clock_code)[0]
    return (result, merged)

def block_backward(out_grad, merged, skip_rows, w_first, w_second, w_clock, w_merge, clock_code):
    result, widened, scale, normed, preact, hidden = inner_block(merged, w_first, w_second, w_clock, clock_code)
    grad_second = contract_rows(hidden, out_grad)
    hidden_grad = contract_cols(out_grad, w_second)
    pre_grad = jax.vjp(gelu_tanh, preact)[1](hidden_grad)[0].astype(jnp.bfloat16)
    grad_first = contract_rows(normed, pre_grad)
    grad_clock = clock_code.astype(jnp.float32)[:, None] * lax.optimization_barrier(jnp.sum(pre_grad.astype(jnp.float32), axis=0))[None, :]
    norm_grad = contract_cols(pre_grad, w_first)
    unit = widened * scale
    merged_grad = (out_grad.astype(jnp.float32) + scale * (norm_grad - unit * lax.optimization_barrier(jnp.mean(norm_grad * unit, axis=-1, keepdims=True)))).astype(jnp.bfloat16)
    grad_merge = contract_rows(skip_rows, merged_grad)
    skip_grad = contract_cols(merged_grad, w_merge).astype(jnp.bfloat16)
    return (merged_grad, skip_grad, (grad_first, grad_second, grad_clock, grad_merge))

def reference(latents, steps, cotangent, w_in, w_out, w_time, w_skip):
    half = N_SECTION // 2
    blank = jnp.zeros((R_DEV, C), jnp.bfloat16)
    outputs = [[[] for batch in range(M)] for section in range(N_SECTION)]
    totals = [[jnp.zeros(w_in.shape[1:], jnp.float32), jnp.zeros(w_out.shape[1:], jnp.float32), jnp.zeros(w_time.shape[1:], jnp.float32), jnp.zeros(w_skip.shape[1:], jnp.float32)] for section in range(N_SECTION)]
    for replica in range(N_DP):
        start_row = replica * R_DEV
        for batch in range(M):
            clock_code = embed(steps[replica, batch], C)
            arriving = latents[batch, start_row:start_row + R_DEV]
            results = []
            merged_list = []
            skip_list = []
            for section in range(N_SECTION):
                skip_rows = results[N_SECTION - 1 - section] if section >= half else blank
                result, merged = block_forward(arriving, skip_rows, w_in[section], w_out[section], w_time[section], w_skip[section], clock_code)
                results.append(result)
                merged_list.append(merged)
                skip_list.append(skip_rows)
                outputs[section][batch].append(result)
                arriving = result
            gradient = cotangent[batch, start_row:start_row + R_DEV]
            returned = {}
            for section in reversed(range(N_SECTION)):
                if section < half:
                    out_grad = (gradient.astype(jnp.float32) + returned[section].astype(jnp.float32)).astype(jnp.bfloat16)
                else:
                    out_grad = gradient
                merged_grad, skip_grad, parts = block_backward(out_grad, merged_list[section], skip_list[section], w_in[section], w_out[section], w_time[section], w_skip[section], clock_code)
                for which in range(4):
                    totals[section][which] = totals[section][which] + parts[which]
                if section >= half:
                    returned[N_SECTION - 1 - section] = skip_grad
                gradient = merged_grad
    section_out = jnp.stack([jnp.stack([jnp.concatenate(outputs[section][batch], axis=0) for batch in range(M)]) for section in range(N_SECTION)])
    grad_w_in = jnp.stack([totals[section][0] for section in range(N_SECTION)])
    grad_w_out = jnp.stack([totals[section][1] for section in range(N_SECTION)])
    grad_w_time = jnp.stack([totals[section][2] for section in range(N_SECTION)])
    grad_w_skip = jnp.stack([totals[section][3] for section in range(N_SECTION)])
    return (section_out, grad_w_in, grad_w_out, grad_w_time, grad_w_skip)
```

```python
import functools
import math

import jax
import jax.numpy as jnp
from jax import lax
from jax.experimental import pallas as pl
from jax.experimental.pallas import tpu as pltpu
from jax.sharding import PartitionSpec as P

MESH = pl.DeviceIdType.MESH
F32 = jnp.float32
BF16 = jnp.bfloat16

SECTIONS = 16
HALF = 8
DP = 8
Z = 4
C = 320
F = 1280
MICRO = 4
HEIGHT = 128
ROWS = MICRO * HEIGHT
R = 64
N = ROWS // R
PER = HEIGHT // R
WIDE = 1664
CPAD = 384
GELU_C = math.sqrt(2.0 / math.pi)


def embed(step_value, width):
    half_width = width // 2
    position = jnp.arange(half_width).astype(F32)
    frequency = jnp.exp(-math.log(10000.0) * position / half_width)
    angle = step_value.astype(F32) * frequency
    return jnp.concatenate([jnp.sin(angle), jnp.cos(angle)]).astype(BF16)


def dot_nn(a, b):
    return lax.dot_general(a, b, (((1,), (0,)), ((), ())), preferred_element_type=F32)


def dot_nt(a, b):
    return lax.dot_general(a, b, (((1,), (1,)), ((), ())), preferred_element_type=F32)


def dot_tn(a, b):
    return lax.dot_general(a, b, (((0,), (0,)), ((), ())), preferred_element_type=F32)


class Item:
    def __init__(self, half_rows, half_cols, by_cols, out, refs, sems):
        self.half_rows = half_rows
        self.half_cols = half_cols
        self.by_cols = by_cols
        self.quarter = half_rows // Z
        self.out = out
        self.psend, self.precv, self.acc, self.zsend, self.zrecv = refs
        (self.ps, self.pr, self.zs, self.zr, self.gs, self.gr, self.fs, self.fr) = sems

    def place(self, core, z):
        if self.by_cols:
            return self.out.at[
                pl.ds(pl.multiple_of(z * self.quarter, 16), self.quarter),
                pl.ds(pl.multiple_of(core * self.half_cols, 128), self.half_cols),
            ]
        start = pl.multiple_of(core * self.half_rows + z * self.quarter, 16)
        return self.out.at[pl.ds(start, self.quarter), :]

    def rows(self, z):
        return pl.ds(pl.multiple_of(z * self.quarter, 16), self.quarter)


def kernel(
    lat, clk, cot, w1, w2, wt, ws,
    out, ga, gb, gc, trow,
    xin, skip, gin, gskip,
    merged, unit, scale, normed, hid, dg, pg, og, mg, sg, bias, gcfull,
    a_ps, a_pr, a_acc, a_zs, a_zr,
    b_ps, b_pr, b_acc, b_zs, b_zr,
    c_ps, c_pr, c_acc, c_zs, c_zr,
    fwd_s, fwd_r, skip_s, skip_r, bwd_s, bwd_r, gsk_s, gsk_r,
    a_sp, a_rp, a_sz, a_rz, a_sg, a_rg, a_sf, a_rf,
    b_sp, b_rp, b_sz, b_rz, b_sg, b_rg, b_sf, b_rf,
    c_sp, c_rp, c_sz, c_rz, c_sg, c_rg, c_sf, c_rf,
    t_s, t_r,
):
    sec = lax.axis_index("section")
    dp = lax.axis_index("dp")
    core = lax.rem(dp, 2)
    zed = lax.div(dp, 2)
    nxt = lax.rem(sec + 1, SECTIONS)
    prv = lax.rem(sec + SECTIONS - 1, SECTIONS)
    mirror = SECTIONS - 1 - sec
    partner = zed * 2 + (1 - core)
    peers = [lax.rem(zed + k, Z) * 2 + core for k in range(1, Z)]

    barrier = pltpu.get_barrier_semaphore()
    for where in (nxt, prv, mirror):
        pl.semaphore_signal(barrier, inc=1, device_id=(where, dp), device_id_type=MESH)
    for k in range(1, DP):
        pl.semaphore_signal(
            barrier, inc=1, device_id=(sec, lax.rem(dp + k, DP)), device_id_type=MESH
        )

    def remote(src, dst, ssem, rsem, section, replica):
        return pltpu.make_async_remote_copy(
            src_ref=src, dst_ref=dst, send_sem=ssem, recv_sem=rsem,
            device_id=(section, replica), device_id_type=MESH,
        )

    bias[...] = dot_nn(clk[...].astype(BF16), wt[...])
    pl.semaphore_wait(barrier, 10)

    def chunk(c):
        return pl.ds(pl.multiple_of(c * R, R), R)

    def send_out(c):
        return remote(out.at[chunk(c), :], xin.at[chunk(c), :], fwd_s.at[c], fwd_r.at[c], nxt, dp)

    def send_skip(c):
        return remote(out.at[chunk(c), :], skip.at[chunk(c), :], skip_s.at[c], skip_r.at[c], mirror, dp)

    def send_grad(c):
        return remote(mg.at[chunk(c), :], gin.at[chunk(c), :], bwd_s.at[c], bwd_r.at[c], prv, dp)

    def send_skip_grad(c):
        return remote(sg.at[chunk(c), :], gskip.at[chunk(c), :], gsk_s.at[c], gsk_r.at[c], mirror, dp)

    def forward(c):
        rows = chunk(c)

        @pl.when(sec == 0)
        def _():
            merged[rows, :] = lat[rows, :]

        @pl.when(sec > 0)
        def _():
            send_out(c).wait_recv()

        @pl.when((sec > 0) & (sec < HALF))
        def _():
            merged[rows, :] = xin[rows, :]

        @pl.when(sec == HALF)
        def _():
            skip[rows, :] = xin[rows, :]

        @pl.when(sec > HALF)
        def _():
            send_skip(c).wait_recv()

        @pl.when(sec >= HALF)
        def _():
            total = xin[rows, :].astype(F32) + dot_nn(skip[rows, :], ws[...])
            merged[rows, :] = total.astype(BF16)

        wide = merged[rows, :].astype(F32)
        factor = lax.rsqrt(jnp.mean(wide * wide, axis=-1, keepdims=True) + 1e-05)
        one = wide * factor
        norm = one.astype(BF16)
        pre = dot_nn(norm, w1[...]) + bias[pl.ds(lax.div(c, PER), 1), :]
        square = pre * pre
        t = jnp.tanh(pre * (GELU_C + (GELU_C * 0.044715) * square))
        gate = 0.5 + 0.5 * t
        hidden = (pre * gate).astype(BF16)
        result = (wide + dot_nn(hidden, w2[...])).astype(BF16)
        out[rows, :] = result

        @pl.when(sec < SECTIONS - 1)
        def _():
            send_out(c).start()

        @pl.when(sec < HALF - 1)
        def _():
            send_skip(c).start()

        hid[rows, :] = hidden
        normed[rows, :] = norm
        unit[rows, :] = one
        scale[rows, :] = factor
        slope = (0.5 * pre) * (1.0 - t * t) * (GELU_C + (3.0 * GELU_C * 0.044715) * square)
        dg[rows, :] = gate + slope

    def backward(c):
        rows = chunk(c)

        @pl.when(sec == SECTIONS - 1)
        def _():
            og[rows, :] = cot[rows, :]

        @pl.when(sec < SECTIONS - 1)
        def _():
            send_grad(c).wait_recv()

        @pl.when((sec >= HALF) & (sec < SECTIONS - 1))
        def _():
            og[rows, :] = gin[rows, :]

        @pl.when(sec < HALF)
        def _():
            send_skip_grad(c).wait_recv()
            og[rows, :] = (gin[rows, :].astype(F32) + gskip[rows, :].astype(F32)).astype(BF16)

        grad = og[rows, :]
        pre_grad = (dot_nt(grad, w2[...]) * dg[rows, :]).astype(BF16)
        norm_grad = dot_nt(pre_grad, w1[...])
        one = unit[rows, :]
        inner = jnp.mean(norm_grad * one, axis=-1, keepdims=True)
        merged_grad = (grad.astype(F32) + scale[rows, :] * (norm_grad - one * inner)).astype(BF16)
        mg[rows, :] = merged_grad

        @pl.when(sec > 0)
        def _():
            send_grad(c).start()

        @pl.when(sec >= HALF)
        def _():
            sg[rows, :] = dot_nt(merged_grad, ws[...]).astype(BF16)
            send_skip_grad(c).start()

        pg[rows, :] = pre_grad

    delay = jnp.minimum((SECTIONS - 1 - sec) * 6, N)

    def tick(t, carry):
        @pl.when(t < N)
        def _():
            forward(t)

        @pl.when((t >= delay) & (t < N + delay))
        def _():
            backward(t - delay)

        return carry

    lax.fori_loop(0, 2 * N, tick, 0)

    item_a = Item(F // 2, C, False, ga, (a_ps, a_pr, a_acc, a_zs, a_zr),
                  (a_sp, a_rp, a_sz, a_rz, a_sg, a_rg, a_sf, a_rf))
    item_b = Item(C, F // 2, True, gb, (b_ps, b_pr, b_acc, b_zs, b_zr),
                  (b_sp, b_rp, b_sz, b_rz, b_sg, b_rg, b_sf, b_rf))
    item_c = Item(CPAD // 2, C, False, gc, (c_ps, c_pr, c_acc, c_zs, c_zr),
                  (c_sp, c_rp, c_sz, c_rz, c_sg, c_rg, c_sf, c_rf))

    def part_a(k):
        columns = pl.ds(pl.multiple_of(k * (F // 2), 128), F // 2)
        return dot_tn(hid[:, columns], og[...])

    def part_b(k):
        columns = pl.ds(pl.multiple_of(k * (F // 2), 128), F // 2)
        return dot_tn(normed[...], pg[:, columns])

    def part_c(k):
        return gcfull[pl.ds(pl.multiple_of(k * (CPAD // 2), 16), CPAD // 2), :]

    def pair_send(item):
        return remote(item.psend, item.precv, item.ps.at[0], item.pr.at[0], sec, partner)

    def pair_start(item, part):
        item.psend[...] = part(1 - core).astype(BF16)
        pair_send(item).start()

    def z_send(item, k):
        target = lax.rem(zed + k, Z)
        return remote(item.zsend.at[item.rows(target), :], item.zrecv.at[k - 1],
                      item.zs.at[k - 1], item.zr.at[k - 1], sec, peers[k - 1])

    def z_start(item, part):
        item.acc[...] = part(core)
        pair_send(item).wait_recv()
        total = item.acc[...] + item.precv[...].astype(F32)
        item.acc[...] = total
        item.zsend[...] = total.astype(BF16)
        for k in range(1, Z):
            z_send(item, k).start()

    def gather_send(item, k):
        spot = item.place(core, zed)
        return remote(spot, spot, item.gs.at[k - 1], item.gr.at[k - 1], sec, peers[k - 1])

    def gather_recv(item, k):
        spot = item.place(core, lax.rem(zed + Z - k, Z))
        return remote(spot, spot, item.gs.at[k - 1], item.gr.at[k - 1], sec, peers[k - 1])

    def pass_send(item, k):
        spot = item.place(core, lax.rem(zed + Z - k, Z))
        return remote(spot, spot, item.fs.at[k], item.fr.at[k], sec, partner)

    def pass_recv(item, k):
        spot = item.place(1 - core, lax.rem(zed + Z - k, Z))
        return remote(spot, spot, item.fs.at[k], item.fr.at[k], sec, partner)

    def gather_start(item):
        for k in range(1, Z):
            z_send(item, k).wait_recv()
        total = item.acc[item.rows(zed), :]
        for k in range(1, Z):
            total = total + item.zrecv[k - 1].astype(F32)
        item.place(core, zed)[...] = total.astype(BF16)
        for k in range(1, Z):
            gather_send(item, k).start()
        pass_send(item, 0).start()

    def pass_start(item):
        for k in (1, 3, 2):
            gather_recv(item, k).wait_recv()
            pass_send(item, k).start()

    def finish(item):
        for k in range(Z):
            pass_recv(item, k).wait_recv()
        pair_send(item).wait_send()
        for k in range(1, Z):
            z_send(item, k).wait_send()
            gather_send(item, k).wait_send()
        for k in range(Z):
            pass_send(item, k).wait_send()

    def time_send(k):
        return remote(trow.at[dp], trow.at[dp], t_s.at[k - 1], t_r.at[k - 1], sec, lax.rem(dp + k, DP))

    def time_recv(k):
        spot = trow.at[lax.rem(dp + DP - k, DP)]
        return remote(spot, spot, t_s.at[k - 1], t_r.at[k - 1], sec, lax.rem(dp + k, DP))

    upper = sec >= HALF
    pair_start(item_a, part_a)
    pair_start(item_b, part_b)
    z_start(item_a, part_a)
    z_start(item_b, part_b)

    batch_of_row = lax.div(lax.broadcasted_iota(jnp.int32, (8, ROWS), 1), HEIGHT)
    batch = lax.broadcasted_iota(jnp.int32, (8, ROWS), 0)
    chosen = jnp.where(batch_of_row == batch, 1.0, 0.0).astype(BF16)
    trow[dp, :, 0:F] = dot_nn(chosen, pg[...])
    trow[dp, :, F:WIDE] = clk2wide(clk[...])
    for k in range(1, DP):
        time_send(k).start()

    @pl.when(upper)
    def _():
        gcfull[...] = jnp.zeros_like(gcfull)
        gcfull[0:C, :] = dot_tn(skip[...], mg[...])
        pair_start(item_c, part_c)
        z_start(item_c, part_c)

    gather_start(item_a)
    gather_start(item_b)
    pass_start(item_a)

    @pl.when(upper)
    def _():
        gather_start(item_c)

    pass_start(item_b)

    @pl.when(upper)
    def _():
        pass_start(item_c)
        finish(item_c)

    @pl.when(jnp.logical_not(upper))
    def _():
        gc[...] = jnp.zeros_like(gc)

    for k in range(1, DP):
        time_recv(k).wait_recv()
        time_send(k).wait_send()

    def drain(c, carry):
        @pl.when(sec < SECTIONS - 1)
        def _():
            send_out(c).wait_send()

        @pl.when(sec < HALF - 1)
        def _():
            send_skip(c).wait_send()

        @pl.when(sec > 0)
        def _():
            send_grad(c).wait_send()

        @pl.when(upper)
        def _():
            send_skip_grad(c).wait_send()

        return carry

    lax.fori_loop(0, N, drain, 0)
    finish(item_a)
    finish(item_b)


def clk2wide(clock):
    return jnp.concatenate([clock, jnp.zeros((8, WIDE - F - C), F32)], axis=1)


def item_scratch(rows, cols):
    return [
        pltpu.VMEM((rows, cols), BF16),
        pltpu.VMEM((rows, cols), BF16),
        pltpu.VMEM((rows, cols), F32),
        pltpu.VMEM((rows, cols), BF16),
        pltpu.VMEM((Z - 1, rows // Z, cols), BF16),
    ]


def item_sems():
    counts = (1, 1, 3, 3, 3, 3, 4, 4)
    return [pltpu.SemaphoreType.DMA((count,)) for count in counts]


def local(latents, steps, cotangent, w_in, w_out, w_time, w_skip):
    table = jnp.stack([embed(steps[0, which], C) for which in range(MICRO)]).astype(F32)
    clock = jnp.concatenate([table, jnp.zeros((8 - MICRO, C), F32)], axis=0)
    vmem = pl.BlockSpec(memory_space=pltpu.VMEM)
    rows_c = pltpu.VMEM((ROWS, C), BF16)
    out, ga, gb, gc, trow = pl.pallas_call(
        kernel,
        out_shape=(
            jax.ShapeDtypeStruct((ROWS, C), BF16),
            jax.ShapeDtypeStruct((F, C), BF16),
            jax.ShapeDtypeStruct((C, F), BF16),
            jax.ShapeDtypeStruct((CPAD, C), BF16),
            jax.ShapeDtypeStruct((DP, 8, WIDE), F32),
        ),
        in_specs=[vmem] * 7,
        out_specs=(vmem,) * 5,
        scratch_shapes=[
            rows_c, rows_c, rows_c, rows_c,
            rows_c,
            pltpu.VMEM((ROWS, C), F32),
            pltpu.VMEM((ROWS, 1), F32),
            rows_c,
            pltpu.VMEM((ROWS, F), BF16),
            pltpu.VMEM((ROWS, F), F32),
            pltpu.VMEM((ROWS, F), BF16),
            rows_c, rows_c, rows_c,
            pltpu.VMEM((8, F), F32),
            pltpu.VMEM((CPAD, C), F32),
        ]
        + item_scratch(F // 2, C)
        + item_scratch(C, F // 2)
        + item_scratch(CPAD // 2, C)
        + [pltpu.SemaphoreType.DMA((N,))] * 8
        + item_sems() + item_sems() + item_sems()
        + [pltpu.SemaphoreType.DMA((DP - 1,))] * 2,
        compiler_params=pltpu.CompilerParams(
            collective_id=0, has_side_effects=True, vmem_limit_bytes=60 * 1024 * 1024
        ),
        name="relay",
    )(
        latents.reshape(ROWS, C), clock, cotangent.reshape(ROWS, C),
        w_in[0], w_out[0], w_time[0], w_skip[0],
    )
    flat = trow.reshape(DP * 8, WIDE)
    grad_time = lax.dot_general(
        flat[:, F:F + C], flat[:, :F], (((0,), (0,)), ((), ())),
        precision=lax.Precision.HIGHEST, preferred_element_type=F32,
    )
    upper = lax.axis_index("section") >= HALF
    grad_skip = jnp.where(upper, gc[:C].astype(F32), 0.0)
    return (
        out.reshape(1, MICRO, HEIGHT, C),
        gb.astype(F32)[None], ga.astype(F32)[None], grad_time[None], grad_skip[None],
    )


def solution(mesh):
    placed = (
        P(None, "dp", None),
        P("dp", None),
        P(None, "dp", None),
        P("section", None, None),
        P("section", None, None),
        P("section", None, None),
        P("section", None, None),
    )
    return jax.shard_map(
        local,
        mesh=mesh,
        in_specs=placed,
        out_specs=(
            P("section", None, "dp", None),
            P("section", None, None),
            P("section", None, None),
            P("section", None, None),
            P("section", None, None),
        ),
        check_vma=False,
    )
```

```python
import functools
import math

import jax
import jax.numpy as jnp
from jax import lax
from jax.experimental import pallas as pl
from jax.experimental.pallas import tpu as pltpu
from jax.sharding import PartitionSpec as P

MESH = pl.DeviceIdType.MESH
F32 = jnp.float32
BF16 = jnp.bfloat16

SECTIONS = 16
HALF = 8
DP = 8
Z = 4
C = 320
F = 1280
MICRO = 4
HEIGHT = 128
ROWS = MICRO * HEIGHT
R = 64
N = ROWS // R
PER = HEIGHT // R
WIDE = 1664
CPAD = 384
GELU_C = math.sqrt(2.0 / math.pi)


def dot_nn(a, b):
    return lax.dot_general(a, b, (((1,), (0,)), ((), ())), preferred_element_type=F32)


def dot_nt(a, b):
    return lax.dot_general(a, b, (((1,), (1,)), ((), ())), preferred_element_type=F32)


def dot_tn(a, b):
    return lax.dot_general(a, b, (((0,), (0,)), ((), ())), preferred_element_type=F32)


class Item:
    def __init__(self, half_rows, half_cols, by_cols, out, refs, sems):
        self.half_rows = half_rows
        self.half_cols = half_cols
        self.by_cols = by_cols
        self.quarter = half_rows // Z
        self.out = out
        self.psend, self.precv, self.acc, self.zsend, self.zrecv = refs
        (self.ps, self.pr, self.zs, self.zr, self.gs, self.gr, self.fs, self.fr) = sems

    def place(self, core, z):
        if self.by_cols:
            return self.out.at[
                pl.ds(pl.multiple_of(z * self.quarter, 16), self.quarter),
                pl.ds(pl.multiple_of(core * self.half_cols, 128), self.half_cols),
            ]
        start = pl.multiple_of(core * self.half_rows + z * self.quarter, 16)
        return self.out.at[pl.ds(start, self.quarter), :]

    def rows(self, z):
        return pl.ds(pl.multiple_of(z * self.quarter, 16), self.quarter)


def gelu_parts(pre):
    square = pre * pre
    t = jnp.tanh(pre * (GELU_C + (GELU_C * 0.044715) * square))
    gate = 0.5 + 0.5 * t
    return square, t, gate


def gelu_slope(pre, square, t, gate):
    return gate + (0.5 * pre) * (1.0 - t * t) * (GELU_C + (3.0 * GELU_C * 0.044715) * square)


def normalise(wide):
    factor = lax.rsqrt(jnp.mean(wide * wide, axis=-1, keepdims=True) + 1e-05)
    return factor, wide * factor


def turned(block):
    return jnp.transpose(block.astype(F32)).astype(BF16)


def kernel(
    lat_h, steps, cot_h, w1_h, w2_h, wt_h, ws_h,
    out_t, ga, gb, gc, trow,
    lat, cot_t, cot, w1, w2, ws, wt, bias, clk,
    xin, skip, gin, gskip, obuf, merged, unit, scale, dg, og, mg, sg, cur,
    out, mf, skf, ogf, mgf, normed, hid, pg, gcfull,
    a_ps, a_pr, a_acc, a_zs, a_zr,
    b_ps, b_pr, b_acc, b_zs, b_zr,
    c_ps, c_pr, c_acc, c_zs, c_zr,
    load, fwd_s, fwd_r, skip_s, skip_r, bwd_s, bwd_r, gsk_s, gsk_r,
    own_s, own_r, gw_s, gw_r, bias_s, bias_r,
    a_sp, a_rp, a_sz, a_rz, a_sg, a_rg, a_sf, a_rf,
    b_sp, b_rp, b_sz, b_rz, b_sg, b_rg, b_sf, b_rf,
    c_sp, c_rp, c_sz, c_rz, c_sg, c_rg, c_sf, c_rf,
    t_s, t_r,
):
    sec = lax.axis_index("section")
    dp = lax.axis_index("dp")
    core = lax.rem(dp, 2)
    zed = lax.div(dp, 2)
    row = lax.div(sec, 4)
    col = lax.rem(sec, 4)
    far_row = 3 - row
    upper = sec >= HALF
    lower = sec < HALF
    own = jnp.where(upper, col, 0)
    partner = zed * 2 + (1 - core)
    peers = [lax.rem(zed + k, Z) * 2 + core for k in range(1, Z)]

    loads = [
        pltpu.make_async_copy(w1_h, w1.at[own], load.at[0]),
        pltpu.make_async_copy(w2_h, w2.at[own], load.at[1]),
        pltpu.make_async_copy(ws_h, ws.at[own], load.at[2]),
        pltpu.make_async_copy(wt_h, wt, load.at[3]),
        pltpu.make_async_copy(lat_h, lat, load.at[4]),
        pltpu.make_async_copy(cot_h, cot_t, load.at[5]),
    ]
    for which in (3, 4, 0, 1, 2, 5):
        loads[which].start()

    barrier = pltpu.get_barrier_semaphore()

    def greet(section, replica):
        pl.semaphore_signal(barrier, inc=1, device_id=(section, replica), device_id_type=MESH)

    for k in range(1, DP):
        greet(sec, lax.rem(dp + k, DP))
    for k in range(4):
        greet(far_row * 4 + k, dp)

    @pl.when(lower)
    def _():
        greet(lax.rem(sec + 1, HALF), dp)
        greet(lax.rem(sec + HALF - 1, HALF), dp)

    @pl.when(upper)
    def _():
        for k in range(1, 4):
            greet(row * 4 + lax.rem(col + k, 4), dp)
        greet((5 - row) * 4 + col, dp)

    def remote(src, dst, ssem, rsem, section, replica):
        return pltpu.make_async_remote_copy(
            src_ref=src, dst_ref=dst, send_sem=ssem, recv_sem=rsem,
            device_id=(section, replica), device_id_type=MESH,
        )

    def arrived(spot, rsem):
        remote(spot, spot, rsem, rsem, sec, partner).wait_recv()

    def sent(spot, ssem):
        remote(spot, spot, ssem, ssem, sec, partner).wait_send()

    batch = lax.broadcasted_iota(jnp.int32, (8, C // 2), 0)
    step = jnp.zeros((8, C // 2), F32)
    for m in range(MICRO):
        step = jnp.where(batch == m, steps[0, m].astype(F32), step)
    place = lax.broadcasted_iota(jnp.int32, (8, C // 2), 1).astype(F32)
    angle = step * jnp.exp(-math.log(10000.0) * place / (C // 2))
    real = batch < MICRO
    clk[:, 0:C // 2] = jnp.where(real, jnp.sin(angle), 0.0).astype(BF16)
    clk[:, C // 2:C] = jnp.where(real, jnp.cos(angle), 0.0).astype(BF16)
    loads[3].wait()
    bias[own] = dot_nn(clk[...], wt[...])
    for which in (4, 0, 1, 2, 5):
        loads[which].wait()

    @pl.when(lower)
    def _():
        pl.semaphore_wait(barrier, 13)

    @pl.when(upper)
    def _():
        pl.semaphore_wait(barrier, 15)

    def chunk(c):
        return pl.ds(pl.multiple_of(c * R, R), R)

    def micro(c):
        return lax.div(c, PER)

    def lower_forward(c, carry):
        rows = chunk(c)

        @pl.when((sec == 0) & (lax.rem(c, PER) == 0))
        def _():
            m = micro(c)
            xin[pl.ds(pl.multiple_of(m * HEIGHT, HEIGHT), HEIGHT), :] = turned(lat[m])

        @pl.when(sec > 0)
        def _():
            arrived(xin.at[rows, :], fwd_r.at[c])

        wide = xin[rows, :].astype(F32)
        factor, one = normalise(wide)
        norm = one.astype(BF16)
        pre = dot_nn(norm, w1[0]) + bias[0, pl.ds(micro(c), 1), :]
        square, t, gate = gelu_parts(pre)
        hidden = (pre * gate).astype(BF16)
        out[rows, :] = (wide + dot_nt(hidden, w2[0])).astype(BF16)

        @pl.when(sec < HALF - 1)
        def _():
            remote(out.at[rows, :], xin.at[rows, :], fwd_s.at[c], fwd_r.at[c], sec + 1, dp).start()
            cell = lax.div(c, 4) * 4 + (3 - col)
            remote(out.at[rows, :], skip.at[chunk(cell), :], skip_s.at[c], skip_r.at[cell],
                   far_row * 4 + lax.rem(c, 4), dp).start()

        @pl.when(sec == HALF - 1)
        def _():
            i = lax.div(c, 4)
            remote(out.at[rows, :], xin.at[chunk(i), :], fwd_s.at[c], fwd_r.at[i],
                   HALF + lax.rem(c, 4), dp).start()

        hid[rows, :] = hidden
        normed[rows, :] = norm
        unit[rows, :] = one
        scale[rows, :] = factor
        dg[rows, :] = gelu_slope(pre, square, t, gate)
        return carry

    def lower_backward(c, carry):
        rows = chunk(c)
        arrived(gskip.at[rows, :], gsk_r.at[c])
        arrived(gin.at[rows, :], bwd_r.at[c])
        grad = (gin[rows, :].astype(F32) + gskip[rows, :].astype(F32)).astype(BF16)
        pre_grad = (dot_nn(grad, w2[0]) * dg[rows, :]).astype(BF16)

        @pl.when(sec > 0)
        def _():
            norm_grad = dot_nt(pre_grad, w1[0])
            one = unit[rows, :]
            inner = jnp.mean(norm_grad * one, axis=-1, keepdims=True)
            mg[rows, :] = (grad.astype(F32) + scale[rows, :] * (norm_grad - one * inner)).astype(BF16)
            remote(mg.at[rows, :], gin.at[rows, :], bwd_s.at[c], bwd_r.at[c], sec - 1, dp).start()

        ogf[rows, :] = grad
        pg[rows, :] = pre_grad
        return carry

    def gather_weights():
        arrays = ((w1, C // 4), (w2, C // 4), (ws, C // 4))
        to_right = row * 4 + lax.rem(col + 1, 4)
        to_left = row * 4 + lax.rem(col + 3, 4)
        left, right, far = lax.rem(col + 3, 4), lax.rem(col + 1, 4), lax.rem(col + 2, 4)

        def piece(which, slot, half, q):
            size = arrays[which][1]
            start = pl.multiple_of(half * (2 * size) + q * size, 16)
            return arrays[which][0].at[slot, pl.ds(start, size), :]

        def move(which, slot, half, q, n, section, replica):
            spot = piece(which, slot, half, q)
            return remote(spot, spot, gw_s.at[which, n], gw_r.at[which, n], section, replica)

        passed = ((left, 0), (left, 1), (right, 0), (right, 1), (far, 0), (far, 1))

        def forward_on(which, n):
            slot, q = passed[n]
            move(which, slot, core, q, 6 + n, sec, partner).start()

        def got(which, n):
            slot, q = passed[n]
            arrived(piece(which, slot, core, q), gw_r.at[which, n])

        for which in range(3):
            move(which, col, core, 0, 0, to_right, dp).start()
            move(which, col, core, 1, 3, to_left, dp).start()
            move(which, col, core, 1, 1, to_right, dp).start()
            move(which, col, core, 0, 2, to_left, dp).start()
        for k in range(1, 4):
            remote(bias.at[col], bias.at[col], bias_s.at[k - 1], bias_r.at[k - 1],
                   row * 4 + lax.rem(col + k, 4), dp).start()
        for which in range(3):
            got(which, 0)
            move(which, left, core, 0, 4, to_right, dp).start()
            forward_on(which, 0)
            got(which, 3)
            move(which, right, core, 1, 5, to_left, dp).start()
            forward_on(which, 3)
            for n in (1, 2):
                got(which, n)
                forward_on(which, n)
        for which in range(3):
            for n in (4, 5):
                got(which, n)
                forward_on(which, n)
        for which in range(3):
            for n in range(6):
                slot, q = passed[n]
                arrived(piece(which, slot, 1 - core, q), gw_r.at[which, 6 + n])
        for k in range(1, 4):
            arrived(bias.at[lax.rem(col + 4 - k, 4)], bias_r.at[k - 1])
        for which in range(3):
            for n in range(12):
                sent(piece(which, col, core, 0), gw_s.at[which, n])
        for k in range(3):
            sent(bias.at[col], bias_s.at[k])

    def give(kind, buffer, cell, full, j, c):
        @pl.when(j == col)
        def _():
            full[chunk(c), :] = buffer[chunk(cell), :]

        @pl.when(j != col)
        def _():
            remote(buffer.at[chunk(cell), :], full.at[chunk(c), :], own_s.at[kind, cell],
                   own_r.at[kind, c], row * 4 + j, dp).start()

    def upper_forward(i):
        c = col + 4 * i
        arrived(xin.at[chunk(i), :], fwd_r.at[i])
        cur[...] = xin[chunk(i), :]

        def layer(j, carry):
            cell = i * 4 + j
            rows = chunk(cell)
            first = (row == 2) & (j == 0)

            @pl.when(first)
            def _():
                skip[rows, :] = cur[...]

            @pl.when(jnp.logical_not(first))
            def _():
                arrived(skip.at[rows, :], skip_r.at[cell])

            total = cur[...].astype(F32) + dot_nn(skip[rows, :], ws[j])
            joined = total.astype(BF16)
            wide = joined.astype(F32)
            factor, one = normalise(wide)
            pre = dot_nn(one.astype(BF16), w1[j]) + bias[j, pl.ds(micro(c), 1), :]
            square, t, gate = gelu_parts(pre)
            hidden = (pre * gate).astype(BF16)
            result = (wide + dot_nt(hidden, w2[j])).astype(BF16)
            obuf[rows, :] = result
            cur[...] = result

            @pl.when((row == 2) & (j == 3))
            def _():
                remote(obuf.at[rows, :], xin.at[chunk(i), :], fwd_s.at[i], fwd_r.at[i], sec + 4, dp).start()

            merged[rows, :] = joined
            unit[rows, :] = one
            scale[rows, :] = factor
            dg[rows, :] = gelu_slope(pre, square, t, gate)
            give(0, obuf, cell, out, j, c)
            give(1, merged, cell, mf, j, c)
            give(2, skip, cell, skf, j, c)
            return carry

        lax.fori_loop(0, 4, layer, 0)

    def upper_backward(i):
        c = col + 4 * i

        @pl.when(row == 3)
        def _():
            cur[...] = cot[chunk(c), :]

        @pl.when(row == 2)
        def _():
            arrived(gin.at[chunk(i), :], bwd_r.at[i])
            cur[...] = gin[chunk(i), :]

        def layer(back, carry):
            j = 3 - back
            cell = i * 4 + j
            rows = chunk(cell)
            grad = cur[...]
            og[rows, :] = grad
            pre_grad = (dot_nn(grad, w2[j]) * dg[rows, :]).astype(BF16)
            norm_grad = dot_nt(pre_grad, w1[j])
            one = unit[rows, :]
            inner = jnp.mean(norm_grad * one, axis=-1, keepdims=True)
            merged_grad = (grad.astype(F32) + scale[rows, :] * (norm_grad - one * inner)).astype(BF16)
            mg[rows, :] = merged_grad
            cur[...] = merged_grad

            @pl.when((row == 3) & (j == 0))
            def _():
                remote(mg.at[rows, :], gin.at[chunk(i), :], bwd_s.at[i], bwd_r.at[i], sec - 4, dp).start()

            @pl.when((row == 2) & (j == 0))
            def _():
                remote(mg.at[rows, :], gin.at[chunk(c), :], bwd_s.at[i], bwd_r.at[c], HALF - 1, dp).start()

            sg[rows, :] = dot_nt(merged_grad, ws[j]).astype(BF16)
            remote(sg.at[rows, :], gskip.at[chunk(c), :], gsk_s.at[cell], gsk_r.at[c],
                   far_row * 4 + (3 - j), dp).start()
            give(3, og, cell, ogf, j, c)
            give(4, mg, cell, mgf, j, c)
            return carry

        lax.fori_loop(0, 4, layer, 0)

    def upper_again(c, carry):
        rows = chunk(c)

        @pl.when(lax.rem(c, 4) != col)
        def _():
            for kind, full in enumerate((out, mf, skf, ogf, mgf)):
                arrived(full.at[rows, :], own_r.at[kind, c])

        one = normalise(mf[rows, :].astype(F32))[1]
        norm = one.astype(BF16)
        pre = dot_nn(norm, w1[col]) + bias[col, pl.ds(micro(c), 1), :]
        square, t, gate = gelu_parts(pre)
        hid[rows, :] = (pre * gate).astype(BF16)
        normed[rows, :] = norm
        pg[rows, :] = (dot_nn(ogf[rows, :], w2[col]) * gelu_slope(pre, square, t, gate)).astype(BF16)
        return carry

    @pl.when(lower)
    def _():
        lax.fori_loop(0, N, lower_forward, 0)
        lax.fori_loop(0, N, lower_backward, 0)

    @pl.when(upper)
    def _():
        gather_weights()

        @pl.when(row == 3)
        def _():
            for m in range(MICRO):
                cot[m * HEIGHT:(m + 1) * HEIGHT, :] = turned(cot_t[m])

        def turn(s, carry):
            late = row == 3
            is_forward = jnp.where(late, lax.rem(s, 2) == 0, s < 2)
            i = jnp.where(late, lax.div(s, 2), lax.rem(s, 2))

            @pl.when(is_forward)
            def _():
                upper_forward(i)

            @pl.when(jnp.logical_not(is_forward))
            def _():
                upper_backward(i)

            return carry

        lax.fori_loop(0, 4, turn, 0)
        lax.fori_loop(0, N, upper_again, 0)

    item_a = Item(C, F // 2, True, ga, (a_ps, a_pr, a_acc, a_zs, a_zr),
                  (a_sp, a_rp, a_sz, a_rz, a_sg, a_rg, a_sf, a_rf))
    item_b = Item(C, F // 2, True, gb, (b_ps, b_pr, b_acc, b_zs, b_zr),
                  (b_sp, b_rp, b_sz, b_rz, b_sg, b_rg, b_sf, b_rf))
    item_c = Item(CPAD // 2, C, False, gc, (c_ps, c_pr, c_acc, c_zs, c_zr),
                  (c_sp, c_rp, c_sz, c_rz, c_sg, c_rg, c_sf, c_rf))

    def part_a(k):
        columns = pl.ds(pl.multiple_of(k * (F // 2), 128), F // 2)
        return dot_tn(ogf[...], hid[:, columns])

    def part_b(k):
        columns = pl.ds(pl.multiple_of(k * (F // 2), 128), F // 2)
        return dot_tn(normed[...], pg[:, columns])

    def part_c(k):
        return gcfull[pl.ds(pl.multiple_of(k * (CPAD // 2), 16), CPAD // 2), :]

    def pair_send(item):
        return remote(item.psend, item.precv, item.ps.at[0], item.pr.at[0], sec, partner)

    def pair_start(item, part):
        item.psend[...] = part(1 - core).astype(BF16)
        pair_send(item).start()

    def z_send(item, k):
        target = lax.rem(zed + k, Z)
        return remote(item.zsend.at[item.rows(target), :], item.zrecv.at[k - 1],
                      item.zs.at[k - 1], item.zr.at[k - 1], sec, peers[k - 1])

    def z_start(item, part):
        item.acc[...] = part(core)
        pair_send(item).wait_recv()
        total = item.acc[...] + item.precv[...].astype(F32)
        item.acc[...] = total
        item.zsend[...] = total.astype(BF16)
        for k in range(1, Z):
            z_send(item, k).start()

    def gather_send(item, k):
        spot = item.place(core, zed)
        return remote(spot, spot, item.gs.at[k - 1], item.gr.at[k - 1], sec, peers[k - 1])

    def gather_recv(item, k):
        spot = item.place(core, lax.rem(zed + Z - k, Z))
        return remote(spot, spot, item.gs.at[k - 1], item.gr.at[k - 1], sec, peers[k - 1])

    def pass_send(item, k):
        spot = item.place(core, lax.rem(zed + Z - k, Z))
        return remote(spot, spot, item.fs.at[k], item.fr.at[k], sec, partner)

    def pass_recv(item, k):
        spot = item.place(1 - core, lax.rem(zed + Z - k, Z))
        return remote(spot, spot, item.fs.at[k], item.fr.at[k], sec, partner)

    def gather_start(item):
        for k in range(1, Z):
            z_send(item, k).wait_recv()
        total = item.acc[item.rows(zed), :]
        for k in range(1, Z):
            total = total + item.zrecv[k - 1].astype(F32)
        item.place(core, zed)[...] = total.astype(BF16)
        for k in range(1, Z):
            gather_send(item, k).start()
        pass_send(item, 0).start()

    def pass_start(item):
        for k in (1, 3, 2):
            gather_recv(item, k).wait_recv()
            pass_send(item, k).start()

    def finish(item):
        for k in range(Z):
            pass_recv(item, k).wait_recv()
        pair_send(item).wait_send()
        for k in range(1, Z):
            z_send(item, k).wait_send()
            gather_send(item, k).wait_send()
        for k in range(Z):
            pass_send(item, k).wait_send()

    def time_send(k):
        return remote(trow.at[dp], trow.at[dp], t_s.at[k - 1], t_r.at[k - 1], sec, lax.rem(dp + k, DP))

    def time_recv(k):
        spot = trow.at[lax.rem(dp + DP - k, DP)]
        return remote(spot, spot, t_s.at[k - 1], t_r.at[k - 1], sec, lax.rem(dp + k, DP))

    pair_start(item_a, part_a)
    pair_start(item_b, part_b)
    z_start(item_a, part_a)
    z_start(item_b, part_b)

    batch_of_row = lax.div(lax.broadcasted_iota(jnp.int32, (8, ROWS), 1), HEIGHT)
    batch_of_sum = lax.broadcasted_iota(jnp.int32, (8, ROWS), 0)
    chosen = jnp.where(batch_of_row == batch_of_sum, 1.0, 0.0).astype(BF16)
    trow[dp, :, 0:F] = dot_nn(chosen, pg[...])
    trow[dp, :, F:WIDE] = clk2wide(clk[...].astype(F32))
    for k in range(1, DP):
        time_send(k).start()

    @pl.when(upper)
    def _():
        gcfull[...] = jnp.zeros_like(gcfull)
        gcfull[0:C, :] = dot_tn(skf[...], mgf[...])
        pair_start(item_c, part_c)
        z_start(item_c, part_c)

    gather_start(item_a)
    gather_start(item_b)
    pass_start(item_a)

    @pl.when(upper)
    def _():
        gather_start(item_c)

    pass_start(item_b)

    @pl.when(upper)
    def _():
        pass_start(item_c)
        finish(item_c)

    @pl.when(jnp.logical_not(upper))
    def _():
        gc[...] = jnp.zeros_like(gc)

    for m in range(MICRO):
        out_t[m] = turned(out[m * HEIGHT:(m + 1) * HEIGHT, :])

    for k in range(1, DP):
        time_recv(k).wait_recv()
        time_send(k).wait_send()

    some = xin.at[chunk(0), :]

    @pl.when(lower)
    def _():
        def drain(c, carry):
            sent(some, fwd_s.at[c])

            @pl.when(sec < HALF - 1)
            def _():
                sent(some, skip_s.at[c])

            @pl.when(sec > 0)
            def _():
                sent(some, bwd_s.at[c])

            return carry

        lax.fori_loop(0, N, drain, 0)

    @pl.when(upper)
    def _():
        def drain(cell, carry):
            sent(some, gsk_s.at[cell])

            @pl.when(lax.rem(cell, 4) != col)
            def _():
                for kind in range(5):
                    sent(some, own_s.at[kind, cell])

            return carry

        lax.fori_loop(0, N, drain, 0)
        for i in range(2):
            sent(some, bwd_s.at[i])

            @pl.when(row == 2)
            def _():
                sent(some, fwd_s.at[i])

    finish(item_a)
    finish(item_b)


def clk2wide(clock):
    return jnp.concatenate([clock, jnp.zeros((8, WIDE - F - C), F32)], axis=1)


def item_scratch(rows, cols):
    return [
        pltpu.VMEM((rows, cols), BF16),
        pltpu.VMEM((rows, cols), BF16),
        pltpu.VMEM((rows, cols), F32),
        pltpu.VMEM((rows, cols), BF16),
        pltpu.VMEM((Z - 1, rows // Z, cols), BF16),
    ]


def item_sems():
    counts = (1, 1, 3, 3, 3, 3, 4, 4)
    return [pltpu.SemaphoreType.DMA((count,)) for count in counts]


def local(latents, steps, cotangent, w_in, w_out, w_time, w_skip):
    vmem = pl.BlockSpec(memory_space=pltpu.VMEM)
    anywhere = pl.BlockSpec(memory_space=pl.ANY)
    rows_c = pltpu.VMEM((ROWS, C), BF16)
    rows_f = pltpu.VMEM((ROWS, F), BF16)
    dma = pltpu.SemaphoreType.DMA
    out_t, ga, gb, gc, trow = pl.pallas_call(
        kernel,
        out_shape=(
            jax.ShapeDtypeStruct((MICRO, C, HEIGHT), BF16),
            jax.ShapeDtypeStruct((C, F), BF16),
            jax.ShapeDtypeStruct((C, F), BF16),
            jax.ShapeDtypeStruct((CPAD, C), BF16),
            jax.ShapeDtypeStruct((DP, 8, WIDE), F32),
        ),
        in_specs=[anywhere, pl.BlockSpec(memory_space=pltpu.SMEM)] + [anywhere] * 5,
        out_specs=(vmem,) * 5,
        scratch_shapes=[
            pltpu.VMEM((MICRO, C, HEIGHT), BF16),
            pltpu.VMEM((MICRO, C, HEIGHT), BF16),
            rows_c,
            pltpu.VMEM((4, C, F), BF16),
            pltpu.VMEM((4, C, F), BF16),
            pltpu.VMEM((4, C, C), BF16),
            pltpu.VMEM((C, F), BF16),
            pltpu.VMEM((4, 8, F), F32),
            pltpu.VMEM((8, C), BF16),
            rows_c, rows_c, rows_c, rows_c,
            rows_c, rows_c,
            pltpu.VMEM((ROWS, C), F32),
            pltpu.VMEM((ROWS, 1), F32),
            pltpu.VMEM((ROWS, F), F32),
            rows_c, rows_c, rows_c,
            pltpu.VMEM((R, C), BF16),
            rows_c, rows_c, rows_c, rows_c, rows_c, rows_c,
            rows_f, rows_f,
            pltpu.VMEM((CPAD, C), F32),
        ]
        + item_scratch(C, F // 2)
        + item_scratch(C, F // 2)
        + item_scratch(CPAD // 2, C)
        + [dma((6,))]
        + [dma((N,))] * 8
        + [dma((5, N))] * 2
        + [dma((3, 12))] * 2
        + [dma((3,))] * 2
        + item_sems() + item_sems() + item_sems()
        + [dma((DP - 1,))] * 2,
        compiler_params=pltpu.CompilerParams(
            collective_id=0, has_side_effects=True, vmem_limit_bytes=60 * 1024 * 1024
        ),
        name="relay",
    )(
        jnp.swapaxes(latents, 1, 2), steps, jnp.swapaxes(cotangent, 1, 2),
        w_in[0], jnp.swapaxes(w_out[0], 0, 1), w_time[0], w_skip[0],
    )
    flat = trow.reshape(DP * 8, WIDE)
    grad_time = lax.dot_general(
        flat[:, F:F + C], flat[:, :F], (((0,), (0,)), ((), ())),
        precision=lax.Precision.HIGHEST, preferred_element_type=F32,
    )
    grad_skip = jnp.where(lax.axis_index("section") >= HALF, gc[:C].astype(F32), 0.0)
    return (
        jnp.swapaxes(out_t, 1, 2)[None],
        gb.astype(F32)[None], jnp.swapaxes(ga.astype(F32), 0, 1)[None], grad_time[None], grad_skip[None],
    )


def solution(mesh):
    placed = (
        P(None, "dp", None),
        P("dp", None),
        P(None, "dp", None),
        P("section", None, None),
        P("section", None, None),
        P("section", None, None),
        P("section", None, None),
    )
    return jax.shard_map(
        local,
        mesh=mesh,
        in_specs=placed,
        out_specs=(
            P("section", None, "dp", None),
            P("section", None, None),
            P("section", None, None),
            P("section", None, None),
            P("section", None, None),
        ),
        check_vma=False,
    )
```

```python
import math

import jax
import jax.numpy as jnp
from jax import lax
from jax.experimental import pallas as pl
from jax.experimental.pallas import tpu as pltpu
from jax.sharding import PartitionSpec as P

MESH = pl.DeviceIdType.MESH
F32 = jnp.float32
BF16 = jnp.bfloat16

SECTIONS = 16
HALF = 8
DP = 8
Z = 4
C = 320
F = 1280
MICRO = 4
HEIGHT = 128
ROWS = MICRO * HEIGHT
R = 64
N = ROWS // R
PER = HEIGHT // R
WIDE = 1664
CPAD = 384
BLOCK = 64
GELU_C = math.sqrt(2.0 / math.pi)


def dot_nn(a, b):
    return lax.dot_general(a, b, (((1,), (0,)), ((), ())), preferred_element_type=F32)


def dot_nt(a, b):
    return lax.dot_general(a, b, (((1,), (1,)), ((), ())), preferred_element_type=F32)


def dot_tn(a, b):
    return lax.dot_general(a, b, (((0,), (0,)), ((), ())), preferred_element_type=F32)


class Item:
    def __init__(self, half_rows, half_cols, by_cols, hand, out, refs, sems):
        self.half_rows = half_rows
        self.half_cols = half_cols
        self.by_cols = by_cols
        self.hand = hand
        self.quarter = half_rows // Z
        self.out = out
        self.psend, self.precv, self.acc, self.zsend, self.zrecv, self.comb = refs
        (self.ps, self.pr, self.zs, self.zr, self.gs, self.gr, self.fs, self.fr) = sems

    def place(self, core, z):
        if self.by_cols:
            return self.out.at[
                pl.ds(pl.multiple_of(z * self.quarter, 16), self.quarter),
                pl.ds(pl.multiple_of(core * self.half_cols, 128), self.half_cols),
            ]
        start = pl.multiple_of(core * self.half_rows + z * self.quarter, 16)
        return self.out.at[pl.ds(start, self.quarter), :]

    def rows(self, z):
        return pl.ds(pl.multiple_of(z * self.quarter, 16), self.quarter)


def gelu_parts(pre):
    square = pre * pre
    t = jnp.tanh(pre * (GELU_C + (GELU_C * 0.044715) * square))
    gate = 0.5 + 0.5 * t
    return square, t, gate


def gelu_slope(pre, square, t, gate):
    return gate + (0.5 * pre) * (1.0 - t * t) * (GELU_C + (3.0 * GELU_C * 0.044715) * square)


def normalise(wide):
    factor = lax.rsqrt(jnp.mean(wide * wide, axis=-1, keepdims=True) + 1e-05)
    return factor, wide * factor


def turned(block):
    return jnp.transpose(block.astype(F32)).astype(BF16)


def kernel(
    lat_h, steps, cot_h, w1_h, w2_h, wt_h, ws_h,
    out_t, ga, gb, gc, trow,
    lat, cot_t, cot, w1, w2, ws, wt, bias, clk,
    xin, skip, gin, gskip, obuf, merged, unit, scale, dg, og, mg, sg, cur,
    out, mf, skf, ogf, mgf, normed, hid, pg, gcfull,
    a_ps, a_pr, a_acc, a_zs, a_zr, a_cb,
    b_ps, b_pr, b_acc, b_zs, b_zr, b_cb,
    c_ps, c_pr, c_acc, c_zs, c_zr, c_cb,
    load, fwd_s, fwd_r, skip_s, skip_r, bwd_s, bwd_r, gsk_s, gsk_r,
    own_s, own_r, gw_s, gw_r, bias_s, bias_r,
    a_sp, a_rp, a_sz, a_rz, a_sg, a_rg, a_sf, a_rf,
    b_sp, b_rp, b_sz, b_rz, b_sg, b_rg, b_sf, b_rf,
    c_sp, c_rp, c_sz, c_rz, c_sg, c_rg, c_sf, c_rf,
    t_s, t_r,
):
    sec = lax.axis_index("section")
    dp = lax.axis_index("dp")
    core = lax.rem(dp, 2)
    zed = lax.div(dp, 2)
    row = lax.div(sec, 4)
    col = lax.rem(sec, 4)
    far_row = 3 - row
    upper = sec >= HALF
    lower = sec < HALF
    own = jnp.where(upper, col, 0)
    partner = zed * 2 + (1 - core)
    quarter_at = {d: lax.rem(zed + d + Z, Z) for d in (-1, 0, 1, 2)}
    device_at = {d: quarter_at[d] * 2 + core for d in (-1, 1, 2)}

    loads = [
        pltpu.make_async_copy(w1_h, w1.at[own], load.at[0]),
        pltpu.make_async_copy(w2_h, w2.at[own], load.at[1]),
        pltpu.make_async_copy(ws_h, ws.at[own], load.at[2]),
        pltpu.make_async_copy(wt_h, wt, load.at[3]),
        pltpu.make_async_copy(lat_h, lat, load.at[4]),
        pltpu.make_async_copy(cot_h, cot_t, load.at[5]),
    ]
    for which in (3, 4, 0, 1, 2, 5):
        loads[which].start()

    barrier = pltpu.get_barrier_semaphore()

    def greet(section, replica):
        pl.semaphore_signal(barrier, inc=1, device_id=(section, replica), device_id_type=MESH)

    for k in range(1, DP):
        greet(sec, lax.rem(dp + k, DP))
    for k in range(4):
        greet(far_row * 4 + k, dp)

    @pl.when(lower)
    def _():
        greet(lax.rem(sec + 1, HALF), dp)
        greet(lax.rem(sec + HALF - 1, HALF), dp)

    @pl.when(upper)
    def _():
        for k in range(1, 4):
            greet(row * 4 + lax.rem(col + k, 4), dp)
        greet((5 - row) * 4 + col, dp)

    def remote(src, dst, ssem, rsem, section, replica):
        return pltpu.make_async_remote_copy(
            src_ref=src, dst_ref=dst, send_sem=ssem, recv_sem=rsem,
            device_id=(section, replica), device_id_type=MESH,
        )

    def arrived(spot, rsem):
        remote(spot, spot, rsem, rsem, sec, partner).wait_recv()

    def sent(spot, ssem):
        remote(spot, spot, ssem, ssem, sec, partner).wait_send()

    batch = lax.broadcasted_iota(jnp.int32, (8, C // 2), 0)
    step = jnp.zeros((8, C // 2), F32)
    for m in range(MICRO):
        step = jnp.where(batch == m, steps[0, m].astype(F32), step)
    place = lax.broadcasted_iota(jnp.int32, (8, C // 2), 1).astype(F32)
    angle = step * jnp.exp(-math.log(10000.0) * place / (C // 2))
    real = batch < MICRO
    clk[:, 0:C // 2] = jnp.where(real, jnp.sin(angle), 0.0).astype(BF16)
    clk[:, C // 2:C] = jnp.where(real, jnp.cos(angle), 0.0).astype(BF16)
    def chunk(c):
        return pl.ds(pl.multiple_of(c * R, R), R)

    def micro(c):
        return lax.div(c, PER)

    def send_skip(c):
        cell = lax.div(c, 4) * 4 + (3 - col)
        remote(out.at[chunk(c), :], skip.at[chunk(cell), :], skip_s.at[c], skip_r.at[cell],
               far_row * 4 + lax.rem(c, 4), dp).start()

    def lower_forward(c, carry):
        rows = chunk(c)

        @pl.when((sec == 0) & (lax.rem(c, PER) == 0))
        def _():
            m = micro(c)
            xin[pl.ds(pl.multiple_of(m * HEIGHT, HEIGHT), HEIGHT), :] = turned(lat[m])

        @pl.when(sec > 0)
        def _():
            arrived(xin.at[rows, :], fwd_r.at[c])

        wide = xin[rows, :].astype(F32)
        factor, one = normalise(wide)
        norm = one.astype(BF16)
        pre = dot_nn(norm, w1[0]) + bias[0, pl.ds(micro(c), 1), :]
        square, t, gate = gelu_parts(pre)
        hidden = (pre * gate).astype(BF16)
        out[rows, :] = (wide + dot_nt(hidden, w2[0])).astype(BF16)

        @pl.when(sec < HALF - 1)
        def _():
            remote(out.at[rows, :], xin.at[rows, :], fwd_s.at[c], fwd_r.at[c], sec + 1, dp).start()

        @pl.when((row == 1) & (sec < HALF - 1))
        def _():
            send_skip(c)

        @pl.when(sec == HALF - 1)
        def _():
            i = lax.div(c, 4)
            remote(out.at[rows, :], xin.at[chunk(i), :], fwd_s.at[c], fwd_r.at[i],
                   HALF + lax.rem(c, 4), dp).start()

        hid[rows, :] = hidden
        normed[rows, :] = norm
        unit[rows, :] = one
        scale[rows, :] = factor
        dg[rows, :] = gelu_slope(pre, square, t, gate)
        return carry

    def lower_backward(c, carry):
        rows = chunk(c)
        arrived(gskip.at[rows, :], gsk_r.at[c])
        arrived(gin.at[rows, :], bwd_r.at[c])
        grad = (gin[rows, :].astype(F32) + gskip[rows, :].astype(F32)).astype(BF16)
        pre_grad = (dot_nn(grad, w2[0]) * dg[rows, :]).astype(BF16)

        @pl.when(sec > 0)
        def _():
            norm_grad = dot_nt(pre_grad, w1[0])
            one = unit[rows, :]
            inner = jnp.mean(norm_grad * one, axis=-1, keepdims=True)
            mg[rows, :] = (grad.astype(F32) + scale[rows, :] * (norm_grad - one * inner)).astype(BF16)
            remote(mg.at[rows, :], gin.at[rows, :], bwd_s.at[c], bwd_r.at[c], sec - 1, dp).start()

        ogf[rows, :] = grad
        pg[rows, :] = pre_grad
        return carry

    def gather_weights():
        arrays = ((w1, C // 4), (w2, C // 4), (ws, C // 4))
        to_right = row * 4 + lax.rem(col + 1, 4)
        to_left = row * 4 + lax.rem(col + 3, 4)
        left, right, far = lax.rem(col + 3, 4), lax.rem(col + 1, 4), lax.rem(col + 2, 4)

        def piece(which, slot, half, q):
            size = arrays[which][1]
            start = pl.multiple_of(half * (2 * size) + q * size, 16)
            return arrays[which][0].at[slot, pl.ds(start, size), :]

        def move(which, slot, half, q, n, section, replica):
            spot = piece(which, slot, half, q)
            return remote(spot, spot, gw_s.at[which, n], gw_r.at[which, n], section, replica)

        passed = ((left, 0), (left, 1), (right, 0), (right, 1), (far, 0), (far, 1))

        def forward_on(which, n):
            slot, q = passed[n]
            move(which, slot, core, q, 6 + n, sec, partner).start()

        def got(which, n):
            slot, q = passed[n]
            arrived(piece(which, slot, core, q), gw_r.at[which, n])

        for which in range(3):
            move(which, col, core, 0, 0, to_right, dp).start()
            move(which, col, core, 1, 3, to_left, dp).start()
            move(which, col, core, 1, 1, to_right, dp).start()
            move(which, col, core, 0, 2, to_left, dp).start()
        loads[3].wait()
        bias[col] = dot_nn(clk[...], wt[...])
        for which in (4, 5):
            loads[which].wait()
        for k in range(1, 4):
            remote(bias.at[col], bias.at[col], bias_s.at[k - 1], bias_r.at[k - 1],
                   row * 4 + lax.rem(col + k, 4), dp).start()
        for which in range(3):
            got(which, 0)
            move(which, left, core, 0, 4, to_right, dp).start()
            forward_on(which, 0)
            got(which, 3)
            move(which, right, core, 1, 5, to_left, dp).start()
            forward_on(which, 3)
            for n in (1, 2):
                got(which, n)
                forward_on(which, n)
        for which in range(3):
            for n in (4, 5):
                got(which, n)
                forward_on(which, n)
        for which in range(3):
            for n in range(6):
                slot, q = passed[n]
                arrived(piece(which, slot, 1 - core, q), gw_r.at[which, 6 + n])
        for k in range(1, 4):
            arrived(bias.at[lax.rem(col + 4 - k, 4)], bias_r.at[k - 1])
        for which in range(3):
            for n in range(12):
                sent(piece(which, col, core, 0), gw_s.at[which, n])
        for k in range(3):
            sent(bias.at[col], bias_s.at[k])

    def give(kind, buffer, cell, full, j, c):
        @pl.when(j == col)
        def _():
            full[chunk(c), :] = buffer[chunk(cell), :]

        @pl.when(j != col)
        def _():
            remote(buffer.at[chunk(cell), :], full.at[chunk(c), :], own_s.at[kind, cell],
                   own_r.at[kind, c], row * 4 + j, dp).start()

    def upper_forward(i):
        c = col + 4 * i
        arrived(xin.at[chunk(i), :], fwd_r.at[i])
        cur[...] = xin[chunk(i), :]

        def layer(j, carry):
            cell = i * 4 + j
            rows = chunk(cell)
            first = (row == 2) & (j == 0)

            @pl.when(first)
            def _():
                skip[rows, :] = cur[...]

            @pl.when(jnp.logical_not(first))
            def _():
                arrived(skip.at[rows, :], skip_r.at[cell])

            total = cur[...].astype(F32) + dot_nn(skip[rows, :], ws[j])
            joined = total.astype(BF16)
            wide = joined.astype(F32)
            factor, one = normalise(wide)
            pre = dot_nn(one.astype(BF16), w1[j]) + bias[j, pl.ds(micro(c), 1), :]
            square, t, gate = gelu_parts(pre)
            hidden = (pre * gate).astype(BF16)
            result = (wide + dot_nt(hidden, w2[j])).astype(BF16)
            obuf[rows, :] = result
            cur[...] = result

            @pl.when((row == 2) & (j == 3))
            def _():
                remote(obuf.at[rows, :], xin.at[chunk(i), :], fwd_s.at[i], fwd_r.at[i], sec + 4, dp).start()

            merged[rows, :] = joined
            unit[rows, :] = one
            scale[rows, :] = factor
            dg[rows, :] = gelu_slope(pre, square, t, gate)
            give(0, obuf, cell, out, j, c)
            give(1, merged, cell, mf, j, c)
            give(2, skip, cell, skf, j, c)
            return carry

        lax.fori_loop(0, 4, layer, 0)

    def upper_backward(i):
        c = col + 4 * i

        @pl.when(row == 3)
        def _():
            cur[...] = cot[chunk(c), :]

        @pl.when(row == 2)
        def _():
            arrived(gin.at[chunk(i), :], bwd_r.at[i])
            cur[...] = gin[chunk(i), :]

        def layer(back, carry):
            j = 3 - back
            cell = i * 4 + j
            rows = chunk(cell)
            grad = cur[...]
            og[rows, :] = grad
            pre_grad = (dot_nn(grad, w2[j]) * dg[rows, :]).astype(BF16)
            norm_grad = dot_nt(pre_grad, w1[j])
            one = unit[rows, :]
            inner = jnp.mean(norm_grad * one, axis=-1, keepdims=True)
            merged_grad = (grad.astype(F32) + scale[rows, :] * (norm_grad - one * inner)).astype(BF16)
            mg[rows, :] = merged_grad
            cur[...] = merged_grad

            @pl.when((row == 3) & (j == 0))
            def _():
                remote(mg.at[rows, :], gin.at[chunk(i), :], bwd_s.at[i], bwd_r.at[i], sec - 4, dp).start()

            @pl.when((row == 2) & (j == 0))
            def _():
                remote(mg.at[rows, :], gin.at[chunk(c), :], bwd_s.at[i], bwd_r.at[c], HALF - 1, dp).start()

            sg[rows, :] = dot_nt(merged_grad, ws[j]).astype(BF16)
            remote(sg.at[rows, :], gskip.at[chunk(c), :], gsk_s.at[cell], gsk_r.at[c],
                   far_row * 4 + (3 - j), dp).start()
            give(3, og, cell, ogf, j, c)
            give(4, mg, cell, mgf, j, c)
            return carry

        lax.fori_loop(0, 4, layer, 0)

    def upper_again(c, carry):
        rows = chunk(c)

        @pl.when(lax.rem(c, 4) != col)
        def _():
            for kind, full in enumerate((out, mf, skf, ogf, mgf)):
                arrived(full.at[rows, :], own_r.at[kind, c])

        one = normalise(mf[rows, :].astype(F32))[1]
        norm = one.astype(BF16)
        pre = dot_nn(norm, w1[col]) + bias[col, pl.ds(micro(c), 1), :]
        square, t, gate = gelu_parts(pre)
        hid[rows, :] = (pre * gate).astype(BF16)
        normed[rows, :] = norm
        pg[rows, :] = (dot_nn(ogf[rows, :], w2[col]) * gelu_slope(pre, square, t, gate)).astype(BF16)
        return carry

    @pl.when(lower)
    def _():
        loads[3].wait()
        bias[0] = dot_nn(clk[...], wt[...])
        for which in (4, 0, 1):
            loads[which].wait()
        pl.semaphore_wait(barrier, 13)
        lax.fori_loop(0, N, lower_forward, 0)

        @pl.when(row == 0)
        def _():
            def later(c, carry):
                send_skip(c)
                return carry

            lax.fori_loop(0, N, later, 0)

        for which in (2, 5):
            loads[which].wait()
        lax.fori_loop(0, N, lower_backward, 0)

    @pl.when(upper)
    def _():
        for which in (0, 1, 2):
            loads[which].wait()
        pl.semaphore_wait(barrier, 15)
        gather_weights()

        @pl.when(row == 3)
        def _():
            for m in range(MICRO):
                cot[m * HEIGHT:(m + 1) * HEIGHT, :] = turned(cot_t[m])

        def turn(s, carry):
            late = row == 3
            is_forward = jnp.where(late, lax.rem(s, 2) == 0, s < 2)
            i = jnp.where(late, lax.div(s, 2), lax.rem(s, 2))

            @pl.when(is_forward)
            def _():
                upper_forward(i)

            @pl.when(jnp.logical_not(is_forward))
            def _():
                upper_backward(i)

            return carry

        lax.fori_loop(0, 4, turn, 0)
        lax.fori_loop(0, N, upper_again, 0)

    item_a = Item(C, F // 2, True, 1, ga, (a_ps, a_pr, a_acc, a_zs, a_zr, a_cb),
                  (a_sp, a_rp, a_sz, a_rz, a_sg, a_rg, a_sf, a_rf))
    item_b = Item(C, F // 2, True, -1, gb, (b_ps, b_pr, b_acc, b_zs, b_zr, b_cb),
                  (b_sp, b_rp, b_sz, b_rz, b_sg, b_rg, b_sf, b_rf))
    item_c = Item(CPAD // 2, C, False, 1, gc, (c_ps, c_pr, c_acc, c_zs, c_zr, c_cb),
                  (c_sp, c_rp, c_sz, c_rz, c_sg, c_rg, c_sf, c_rf))

    def part_a(k):
        columns = pl.ds(pl.multiple_of(k * (F // 2), 128), F // 2)
        return dot_tn(ogf[...], hid[:, columns])

    def part_b(k):
        columns = pl.ds(pl.multiple_of(k * (F // 2), 128), F // 2)
        return dot_tn(normed[...], pg[:, columns])

    def part_c(k):
        return gcfull[pl.ds(pl.multiple_of(k * (CPAD // 2), 16), CPAD // 2), :]

    def pair_send(item):
        return remote(item.psend, item.precv, item.ps.at[0], item.pr.at[0], sec, partner)

    def pair_start(item, part):
        item.psend[...] = part(1 - core).astype(BF16)
        pair_send(item).start()

    def z_start(item, part):
        item.acc[...] = part(core)
        pair_send(item).wait_recv()
        total = item.acc[...] + item.precv[...].astype(F32)
        item.acc[...] = total
        item.zsend[...] = total.astype(BF16)
        hand = item.hand
        remote(item.zsend.at[item.rows(quarter_at[2]), :], item.zrecv.at[0],
               item.zs.at[0], item.zr.at[0], sec, device_at[hand]).start()
        remote(item.zsend.at[item.rows(quarter_at[-hand]), :], item.zrecv.at[1],
               item.zs.at[1], item.zr.at[1], sec, device_at[-hand]).start()

    def z_relay(item):
        hand = item.hand
        arrived(item.zrecv.at[0], item.zr.at[0])
        term = item.acc[item.rows(quarter_at[hand]), :] + item.zrecv[0].astype(F32)
        item.comb[...] = term.astype(BF16)
        remote(item.comb, item.zrecv.at[2], item.zs.at[2], item.zr.at[2], sec, device_at[hand]).start()

    def pass_on(item, d, n):
        spot = item.place(core, quarter_at[d])
        remote(spot, spot, item.fs.at[n], item.fr.at[n], sec, partner).start()

    def spread(item, d, n, to):
        spot = item.place(core, quarter_at[d])
        remote(spot, spot, item.gs.at[n], item.gr.at[n], sec, device_at[to]).start()

    def gather_start(item):
        arrived(item.zrecv.at[1], item.zr.at[1])
        arrived(item.zrecv.at[2], item.zr.at[2])
        total = item.acc[item.rows(zed), :] + item.zrecv[1].astype(F32) + item.zrecv[2].astype(F32)
        item.place(core, zed)[...] = total.astype(BF16)
        spread(item, 0, 0, item.hand)
        spread(item, 0, 1, -item.hand)
        pass_on(item, 0, 0)

    def near_pass(item):
        hand = item.hand
        arrived(item.place(core, quarter_at[-hand]), item.gr.at[0])
        spread(item, -hand, 2, hand)
        pass_on(item, -hand, 1)
        arrived(item.place(core, quarter_at[hand]), item.gr.at[1])
        pass_on(item, hand, 2)

    def far_pass(item):
        arrived(item.place(core, quarter_at[2]), item.gr.at[2])
        pass_on(item, 2, 3)

    def finish(item):
        for n, d in enumerate((0, -item.hand, item.hand, 2)):
            arrived(item.place(1 - core, quarter_at[d]), item.fr.at[n])
        pair_send(item).wait_send()
        quarter = item.zrecv.at[0]
        for n in range(3):
            sent(quarter, item.zs.at[n])
            sent(quarter, item.gs.at[n])
        for n in range(4):
            sent(quarter, item.fs.at[n])

    pair_start(item_a, part_a)
    pair_start(item_b, part_b)
    z_start(item_a, part_a)
    z_start(item_b, part_b)

    batch_of_row = lax.div(lax.broadcasted_iota(jnp.int32, (8, ROWS), 1), HEIGHT)
    batch_of_sum = lax.broadcasted_iota(jnp.int32, (8, ROWS), 0)
    chosen = jnp.where(batch_of_row == batch_of_sum, 1.0, 0.0).astype(BF16)
    sums = dot_nn(chosen, pg[...])
    z_relay(item_a)
    z_relay(item_b)
    trow[dp] = jnp.concatenate([sums, clk[...].astype(F32), jnp.zeros((8, WIDE - F - C), F32)], axis=1).astype(BF16)

    def time_move(d, n, replica):
        spot = trow.at[quarter_at[d] * 2 + core]
        return remote(spot, spot, t_s.at[n], t_r.at[n], sec, replica)

    offsets = (1, -1, 2)
    for n, d in enumerate(offsets):
        time_move(0, n, device_at[d]).start()
    time_move(0, 3, partner).start()

    @pl.when(upper)
    def _():
        gcfull[...] = jnp.zeros_like(gcfull)
        gcfull[0:C, :] = dot_tn(skf[...], mgf[...])
        pair_start(item_c, part_c)
        z_start(item_c, part_c)
        z_relay(item_c)

    gather_start(item_a)
    gather_start(item_b)

    for n, d in enumerate(offsets):
        source = -d if d != 2 else 2
        arrived(trow.at[quarter_at[source] * 2 + core], t_r.at[n])
        time_move(source, 4 + n, partner).start()

    near_pass(item_a)
    near_pass(item_b)

    @pl.when(upper)
    def _():
        gather_start(item_c)
        near_pass(item_c)

    for m in range(MICRO):
        out_t[m] = turned(out[m * HEIGHT:(m + 1) * HEIGHT, :])

    far_pass(item_a)
    far_pass(item_b)

    @pl.when(upper)
    def _():
        far_pass(item_c)
        finish(item_c)

    @pl.when(lower)
    def _():
        gc[...] = jnp.zeros_like(gc)

    for n in range(7):
        d = 0 if n < 4 else (-1, 1, 2)[n - 4]
        if n >= 3:
            arrived(trow.at[quarter_at[d] * 2 + (1 - core)], t_r.at[n])
        sent(trow.at[dp], t_s.at[n])

    some = xin.at[chunk(0), :]

    @pl.when(lower)
    def _():
        def drain(c, carry):
            sent(some, fwd_s.at[c])

            @pl.when(sec < HALF - 1)
            def _():
                sent(some, skip_s.at[c])

            @pl.when(sec > 0)
            def _():
                sent(some, bwd_s.at[c])

            return carry

        lax.fori_loop(0, N, drain, 0)

    @pl.when(upper)
    def _():
        def drain(cell, carry):
            sent(some, gsk_s.at[cell])

            @pl.when(lax.rem(cell, 4) != col)
            def _():
                for kind in range(5):
                    sent(some, own_s.at[kind, cell])

            return carry

        lax.fori_loop(0, N, drain, 0)
        for i in range(2):
            sent(some, bwd_s.at[i])

            @pl.when(row == 2)
            def _():
                sent(some, fwd_s.at[i])

    finish(item_a)
    finish(item_b)


def finishing(ga, gb, gc, trow, out_t, a_out, b_out, t_out, s_out, o_out, clock_t):
    upper = lax.axis_index("section") >= HALF
    block = pl.program_id(0)

    @pl.when(block == 0)
    def _():
        clock_t[...] = jnp.transpose(trow[:, F:F + C].astype(F32)).astype(BF16)

    rows = pl.ds(pl.multiple_of(block * BLOCK, BLOCK), BLOCK)
    a_out[...] = ga[...].astype(F32)
    b_out[...] = gb[...].astype(F32)
    t_out[...] = dot_nn(clock_t[rows, :], trow[:, 0:F])
    s_out[...] = jnp.where(upper, gc[...].astype(F32), 0.0)
    o_out[...] = out_t[...]


def item_scratch(rows, cols):
    return [
        pltpu.VMEM((rows, cols), BF16),
        pltpu.VMEM((rows, cols), BF16),
        pltpu.VMEM((rows, cols), F32),
        pltpu.VMEM((rows, cols), BF16),
        pltpu.VMEM((Z - 1, rows // Z, cols), BF16),
        pltpu.VMEM((rows // Z, cols), BF16),
    ]


def item_sems():
    counts = (1, 1, 3, 3, 3, 3, 4, 4)
    return [pltpu.SemaphoreType.DMA((count,)) for count in counts]


def local(latents, steps, cotangent, w_in, w_out, w_time, w_skip):
    vmem = pl.BlockSpec(memory_space=pltpu.VMEM)
    anywhere = pl.BlockSpec(memory_space=pl.ANY)
    rows_c = pltpu.VMEM((ROWS, C), BF16)
    rows_f = pltpu.VMEM((ROWS, F), BF16)
    dma = pltpu.SemaphoreType.DMA
    out_t, ga, gb, gc, trow = pl.pallas_call(
        kernel,
        out_shape=(
            jax.ShapeDtypeStruct((MICRO, C, HEIGHT), BF16),
            jax.ShapeDtypeStruct((C, F), BF16),
            jax.ShapeDtypeStruct((C, F), BF16),
            jax.ShapeDtypeStruct((CPAD, C), BF16),
            jax.ShapeDtypeStruct((DP, 8, WIDE), BF16),
        ),
        in_specs=[anywhere, pl.BlockSpec(memory_space=pltpu.SMEM)] + [anywhere] * 5,
        out_specs=(vmem,) * 5,
        scratch_shapes=[
            pltpu.VMEM((MICRO, C, HEIGHT), BF16),
            pltpu.VMEM((MICRO, C, HEIGHT), BF16),
            rows_c,
            pltpu.VMEM((4, C, F), BF16),
            pltpu.VMEM((4, C, F), BF16),
            pltpu.VMEM((4, C, C), BF16),
            pltpu.VMEM((C, F), BF16),
            pltpu.VMEM((4, 8, F), F32),
            pltpu.VMEM((8, C), BF16),
            rows_c, rows_c, rows_c, rows_c,
            rows_c, rows_c,
            pltpu.VMEM((ROWS, C), F32),
            pltpu.VMEM((ROWS, 1), F32),
            pltpu.VMEM((ROWS, F), F32),
            rows_c, rows_c, rows_c,
            pltpu.VMEM((R, C), BF16),
            rows_c, rows_c, rows_c, rows_c, rows_c, rows_c,
            rows_f, rows_f,
            pltpu.VMEM((CPAD, C), F32),
        ]
        + item_scratch(C, F // 2)
        + item_scratch(C, F // 2)
        + item_scratch(CPAD // 2, C)
        + [dma((6,))]
        + [dma((N,))] * 8
        + [dma((5, N))] * 2
        + [dma((3, 12))] * 2
        + [dma((3,))] * 2
        + item_sems() + item_sems() + item_sems()
        + [dma((DP - 1,))] * 2,
        compiler_params=pltpu.CompilerParams(
            collective_id=0, has_side_effects=True, vmem_limit_bytes=60 * 1024 * 1024
        ),
        name="relay",
    )(
        jnp.swapaxes(latents, 1, 2), steps, jnp.swapaxes(cotangent, 1, 2),
        w_in[0], jnp.swapaxes(w_out[0], 0, 1), w_time[0], w_skip[0],
    )
    wide = pl.BlockSpec((BLOCK, F), lambda i: (i, 0))
    narrow = pl.BlockSpec((BLOCK, C), lambda i: (i, 0))
    turned_rows = pl.BlockSpec((MICRO, BLOCK, HEIGHT), lambda i: (0, i, 0))
    grad_out_t, grad_in, grad_time, grad_skip, out_t = pl.pallas_call(
        finishing,
        grid=(C // BLOCK,),
        out_shape=(
            jax.ShapeDtypeStruct((C, F), F32),
            jax.ShapeDtypeStruct((C, F), F32),
            jax.ShapeDtypeStruct((C, F), F32),
            jax.ShapeDtypeStruct((C, C), F32),
            jax.ShapeDtypeStruct((MICRO, C, HEIGHT), BF16),
        ),
        in_specs=[wide, wide, narrow, pl.BlockSpec((DP * 8, WIDE), lambda i: (0, 0)), turned_rows],
        out_specs=(wide, wide, wide, narrow, turned_rows),
        scratch_shapes=[pltpu.VMEM((C, DP * 8), BF16)],
        name="finishing",
    )(ga, gb, gc, trow.reshape(DP * 8, WIDE), out_t)
    return (
        jnp.swapaxes(out_t, 1, 2)[None],
        grad_in[None], jnp.swapaxes(grad_out_t, 0, 1)[None], grad_time[None], grad_skip[None],
    )


def solution(mesh):
    placed = (
        P(None, "dp", None),
        P("dp", None),
        P(None, "dp", None),
        P("section", None, None),
        P("section", None, None),
        P("section", None, None),
        P("section", None, None),
    )
    return jax.shard_map(
        local,
        mesh=mesh,
        in_specs=placed,
        out_specs=(
            P("section", None, "dp", None),
            P("section", None, None),
            P("section", None, None),
            P("section", None, None),
            P("section", None, None),
        ),
        check_vma=False,
    )
```

```python
import math

import jax
import jax.numpy as jnp
from jax import lax
from jax.experimental import pallas as pl
from jax.experimental.pallas import tpu as pltpu
from jax.sharding import PartitionSpec as P

MESH = pl.DeviceIdType.MESH
F32 = jnp.float32
BF16 = jnp.bfloat16

SECTIONS = 16
HALF = 8
DP = 8
Z = 4
C = 320
F = 1280
MICRO = 4
HEIGHT = 128
ROWS = MICRO * HEIGHT
R = 64
N = ROWS // R
PER = HEIGHT // R
WIDE = 1664
CPAD = 384
BLOCK = 160
GELU_C = math.sqrt(2.0 / math.pi)


def dot_nn(a, b):
    return lax.dot_general(a, b, (((1,), (0,)), ((), ())), preferred_element_type=F32)


def dot_nt(a, b):
    return lax.dot_general(a, b, (((1,), (1,)), ((), ())), preferred_element_type=F32)


def dot_tn(a, b):
    return lax.dot_general(a, b, (((0,), (0,)), ((), ())), preferred_element_type=F32)


class Item:
    def __init__(self, half_rows, half_cols, by_cols, hand, out, refs, sems):
        self.half_rows = half_rows
        self.half_cols = half_cols
        self.by_cols = by_cols
        self.hand = hand
        self.quarter = half_rows // Z
        self.out = out
        self.psend, self.precv, self.acc, self.zsend, self.zrecv, self.comb = refs
        (self.ps, self.pr, self.zs, self.zr, self.gs, self.gr, self.fs, self.fr) = sems

    def place(self, core, z):
        if self.by_cols:
            return self.out.at[
                pl.ds(pl.multiple_of(z * self.quarter, 16), self.quarter),
                pl.ds(pl.multiple_of(core * self.half_cols, 128), self.half_cols),
            ]
        start = pl.multiple_of(core * self.half_rows + z * self.quarter, 16)
        return self.out.at[pl.ds(start, self.quarter), :]

    def rows(self, z):
        return pl.ds(pl.multiple_of(z * self.quarter, 16), self.quarter)


def gelu_parts(pre):
    square = pre * pre
    t = jnp.tanh(pre * (GELU_C + (GELU_C * 0.044715) * square))
    gate = 0.5 + 0.5 * t
    return square, t, gate


def gelu_slope(pre, square, t, gate):
    return gate + (0.5 * pre) * (1.0 - t * t) * (GELU_C + (3.0 * GELU_C * 0.044715) * square)


def normalise(wide):
    factor = lax.rsqrt(jnp.mean(wide * wide, axis=-1, keepdims=True) + 1e-05)
    return factor, wide * factor


def turned(block):
    return jnp.transpose(block.astype(F32)).astype(BF16)


def kernel(
    lat_h, steps, cot_h, w1_h, w2_h, wt_h, ws_h,
    out_t, ga, gb, gc, trow,
    lat, cot_t, cot, w1, w2, ws, wt, bias, clk,
    xin, skip, gin, gskip, obuf, merged, unit, scale, dg, dgo, og, mg, sg, cur,
    out, mf, skf, ogf, mgf, normed, hid, pg, gcfull,
    a_ps, a_pr, a_acc, a_zs, a_zr, a_cb,
    b_ps, b_pr, b_acc, b_zs, b_zr, b_cb,
    c_ps, c_pr, c_acc, c_zs, c_zr, c_cb,
    load, fwd_s, fwd_r, skip_s, skip_r, bwd_s, bwd_r, gsk_s, gsk_r,
    own_s, own_r, in_s, in_r, gw_s, gw_r, bias_s, bias_r,
    a_sp, a_rp, a_sz, a_rz, a_sg, a_rg, a_sf, a_rf,
    b_sp, b_rp, b_sz, b_rz, b_sg, b_rg, b_sf, b_rf,
    c_sp, c_rp, c_sz, c_rz, c_sg, c_rg, c_sf, c_rf,
    t_s, t_r,
):
    sec = lax.axis_index("section")
    dp = lax.axis_index("dp")
    core = lax.rem(dp, 2)
    zed = lax.div(dp, 2)
    row = lax.div(sec, 4)
    col = lax.rem(sec, 4)
    far_row = 3 - row
    upper = sec >= HALF
    lower = sec < HALF
    own = col
    partner = zed * 2 + (1 - core)
    quarter_at = {d: lax.rem(zed + d + Z, Z) for d in (-1, 0, 1, 2)}
    device_at = {d: quarter_at[d] * 2 + core for d in (-1, 1, 2)}

    loads = [
        pltpu.make_async_copy(w1_h, w1.at[own], load.at[0]),
        pltpu.make_async_copy(w2_h, w2.at[own], load.at[1]),
        pltpu.make_async_copy(ws_h, ws.at[own], load.at[2]),
        pltpu.make_async_copy(wt_h, wt, load.at[3]),
        pltpu.make_async_copy(lat_h, lat, load.at[4]),
        pltpu.make_async_copy(cot_h, cot_t, load.at[5]),
    ]
    for which in (3, 4, 0, 1, 2, 5):
        loads[which].start()

    barrier = pltpu.get_barrier_semaphore()

    def greet(section, replica):
        pl.semaphore_signal(barrier, inc=1, device_id=(section, replica), device_id_type=MESH)

    for k in range(1, DP):
        greet(sec, lax.rem(dp + k, DP))
    for k in range(4):
        greet(far_row * 4 + k, dp)

    for k in range(1, 4):
        greet(row * 4 + lax.rem(col + k, 4), dp)
    greet((row + 1 - 2 * lax.rem(row, 2)) * 4 + col, dp)
    bend = (sec == 3) | (sec == 4)

    @pl.when(bend)
    def _():
        greet(7 - sec, dp)

    greetings = jnp.where(bend, 16, 15)

    def remote(src, dst, ssem, rsem, section, replica):
        return pltpu.make_async_remote_copy(
            src_ref=src, dst_ref=dst, send_sem=ssem, recv_sem=rsem,
            device_id=(section, replica), device_id_type=MESH,
        )

    def arrived(spot, rsem):
        remote(spot, spot, rsem, rsem, sec, partner).wait_recv()

    def sent(spot, ssem):
        remote(spot, spot, ssem, ssem, sec, partner).wait_send()

    batch = lax.broadcasted_iota(jnp.int32, (8, C // 2), 0)
    step = jnp.zeros((8, C // 2), F32)
    for m in range(MICRO):
        step = jnp.where(batch == m, steps[0, m].astype(F32), step)
    place = lax.broadcasted_iota(jnp.int32, (8, C // 2), 1).astype(F32)
    angle = step * jnp.exp(-math.log(10000.0) * place / (C // 2))
    real = batch < MICRO
    clk[:, 0:C // 2] = jnp.where(real, jnp.sin(angle), 0.0).astype(BF16)
    clk[:, C // 2:C] = jnp.where(real, jnp.cos(angle), 0.0).astype(BF16)
    def chunk(c):
        return pl.ds(pl.multiple_of(c * R, R), R)

    def micro(c):
        return lax.div(c, PER)

    def send_skip(c):
        cell = lax.div(c, 4) * 4 + (3 - col)
        remote(out.at[chunk(c), :], skip.at[chunk(cell), :], skip_s.at[c], skip_r.at[cell],
               far_row * 4 + lax.rem(c, 4), dp).start()

    def lower_forward(c, carry):
        rows = chunk(c)

        @pl.when(sec > 0)
        def _():
            arrived(xin.at[rows, :], fwd_r.at[c])

        wide = xin[rows, :].astype(F32)
        norm = normalise(wide)[1].astype(BF16)
        pre = dot_nn(norm, w1[col]) + bias[col, pl.ds(micro(c), 1), :]
        square, t, gate = gelu_parts(pre)
        hidden = (pre * gate).astype(BF16)
        out[rows, :] = (wide + dot_nt(hidden, w2[col])).astype(BF16)

        @pl.when(sec < HALF - 1)
        def _():
            remote(out.at[rows, :], xin.at[rows, :], fwd_s.at[c], fwd_r.at[c], sec + 1, dp).start()

        @pl.when((row == 1) & (sec < HALF - 1))
        def _():
            send_skip(c)

        @pl.when(sec == HALF - 1)
        def _():
            i = lax.div(c, 4)
            remote(out.at[rows, :], xin.at[chunk(i), :], fwd_s.at[c], fwd_r.at[i],
                   HALF + lax.rem(c, 4), dp).start()

        hid[rows, :] = hidden
        normed[rows, :] = norm
        dgo[rows, :] = gelu_slope(pre, square, t, gate)
        return carry

    def hand_input(c, carry):
        cell = lax.div(c, 4) * 4 + col
        place_of = lax.rem(c, 4)

        @pl.when(place_of == col)
        def _():
            merged[chunk(cell), :] = xin[chunk(c), :]

        @pl.when(place_of != col)
        def _():
            remote(xin.at[chunk(c), :], merged.at[chunk(cell), :], in_s.at[c], in_r.at[cell],
                   row * 4 + place_of, dp).start()

        return carry

    def lower_prepare(cell, carry):
        j = lax.rem(cell, 4)
        c = col + 4 * lax.div(cell, 4)
        rows = chunk(cell)

        @pl.when(j != col)
        def _():
            arrived(merged.at[rows, :], in_r.at[cell])

        factor, one = normalise(merged[rows, :].astype(F32))
        pre = dot_nn(one.astype(BF16), w1[j]) + bias[j, pl.ds(micro(c), 1), :]
        square, t, gate = gelu_parts(pre)
        unit[rows, :] = one
        scale[rows, :] = factor
        dg[rows, :] = gelu_slope(pre, square, t, gate)
        return carry

    def lower_backward(i):
        c = col + 4 * i
        arrived(gin.at[chunk(i), :], bwd_r.at[i])
        cur[...] = gin[chunk(i), :]

        def layer(back, carry):
            j = 3 - back
            cell = i * 4 + j
            rows = chunk(cell)
            arrived(gskip.at[rows, :], gsk_r.at[cell])
            grad = (cur[...].astype(F32) + gskip[rows, :].astype(F32)).astype(BF16)
            og[rows, :] = grad
            give(3, og, cell, ogf, j, c)
            pre_grad = (dot_nn(grad, w2[j]) * dg[rows, :]).astype(BF16)
            norm_grad = dot_nt(pre_grad, w1[j])
            one = unit[rows, :]
            inner = jnp.mean(norm_grad * one, axis=-1, keepdims=True)
            merged_grad = (grad.astype(F32) + scale[rows, :] * (norm_grad - one * inner)).astype(BF16)
            cur[...] = merged_grad

            @pl.when((row == 1) & (j == 0))
            def _():
                mg[rows, :] = merged_grad
                remote(mg.at[rows, :], gin.at[chunk(i), :], bwd_s.at[i], bwd_r.at[i], sec - 4, dp).start()

            return carry

        lax.fori_loop(0, 4, layer, 0)

    def lower_again(c, carry):
        rows = chunk(c)

        @pl.when(lax.rem(c, 4) != col)
        def _():
            arrived(ogf.at[rows, :], own_r.at[3, c])

        pg[rows, :] = (dot_nn(ogf[rows, :], w2[col]) * dgo[rows, :]).astype(BF16)
        return carry

    def gather(count, opening, closing):
        arrays = ((w1, C // 4), (w2, C // 4), (ws, C // 4))
        to_right = row * 4 + lax.rem(col + 1, 4)
        to_left = row * 4 + lax.rem(col + 3, 4)
        left, right, far = lax.rem(col + 3, 4), lax.rem(col + 1, 4), lax.rem(col + 2, 4)

        def piece(which, slot, half, q):
            size = arrays[which][1]
            start = pl.multiple_of(half * (2 * size) + q * size, 16)
            return arrays[which][0].at[slot, pl.ds(start, size), :]

        def move(which, slot, half, q, n, section, replica):
            spot = piece(which, slot, half, q)
            return remote(spot, spot, gw_s.at[which, n], gw_r.at[which, n], section, replica)

        passed = ((left, 0), (left, 1), (right, 0), (right, 1), (far, 0), (far, 1))

        def forward_on(which, n):
            slot, q = passed[n]
            move(which, slot, core, q, 6 + n, sec, partner).start()

        def got(which, n):
            slot, q = passed[n]
            arrived(piece(which, slot, core, q), gw_r.at[which, n])

        if opening:
            for which in range(count):
                move(which, col, core, 0, 0, to_right, dp).start()
                move(which, col, core, 1, 3, to_left, dp).start()
                move(which, col, core, 1, 1, to_right, dp).start()
                move(which, col, core, 0, 2, to_left, dp).start()
        if not closing:
            return
        for k in range(1, 4):
            remote(bias.at[col], bias.at[col], bias_s.at[k - 1], bias_r.at[k - 1],
                   row * 4 + lax.rem(col + k, 4), dp).start()
        for which in range(count):
            got(which, 0)
            move(which, left, core, 0, 4, to_right, dp).start()
            forward_on(which, 0)
            got(which, 3)
            move(which, right, core, 1, 5, to_left, dp).start()
            forward_on(which, 3)
            for n in (1, 2):
                got(which, n)
                forward_on(which, n)
        for which in range(count):
            for n in (4, 5):
                got(which, n)
                forward_on(which, n)
        for which in range(count):
            for n in range(6):
                slot, q = passed[n]
                arrived(piece(which, slot, 1 - core, q), gw_r.at[which, 6 + n])
        for k in range(1, 4):
            arrived(bias.at[lax.rem(col + 4 - k, 4)], bias_r.at[k - 1])
        for which in range(count):
            for n in range(12):
                sent(piece(which, col, core, 0), gw_s.at[which, n])
        for k in range(3):
            sent(bias.at[col], bias_s.at[k])

    def give(kind, buffer, cell, full, j, c):
        @pl.when(j == col)
        def _():
            full[chunk(c), :] = buffer[chunk(cell), :]

        @pl.when(j != col)
        def _():
            remote(buffer.at[chunk(cell), :], full.at[chunk(c), :], own_s.at[kind, cell],
                   own_r.at[kind, c], row * 4 + j, dp).start()

    def upper_forward(i):
        c = col + 4 * i
        arrived(xin.at[chunk(i), :], fwd_r.at[i])
        cur[...] = xin[chunk(i), :]

        def layer(j, carry):
            cell = i * 4 + j
            rows = chunk(cell)
            first = (row == 2) & (j == 0)

            @pl.when(first)
            def _():
                skip[rows, :] = cur[...]

            @pl.when(jnp.logical_not(first))
            def _():
                arrived(skip.at[rows, :], skip_r.at[cell])

            total = cur[...].astype(F32) + dot_nn(skip[rows, :], ws[j])
            joined = total.astype(BF16)
            wide = joined.astype(F32)
            factor, one = normalise(wide)
            pre = dot_nn(one.astype(BF16), w1[j]) + bias[j, pl.ds(micro(c), 1), :]
            square, t, gate = gelu_parts(pre)
            hidden = (pre * gate).astype(BF16)
            result = (wide + dot_nt(hidden, w2[j])).astype(BF16)
            obuf[rows, :] = result
            cur[...] = result

            @pl.when((row == 2) & (j == 3))
            def _():
                remote(obuf.at[rows, :], xin.at[chunk(i), :], fwd_s.at[i], fwd_r.at[i], sec + 4, dp).start()

            merged[rows, :] = joined
            unit[rows, :] = one
            scale[rows, :] = factor
            dg[rows, :] = gelu_slope(pre, square, t, gate)
            give(0, obuf, cell, out, j, c)
            give(1, merged, cell, mf, j, c)
            give(2, skip, cell, skf, j, c)
            return carry

        lax.fori_loop(0, 4, layer, 0)

    def upper_backward(i):
        c = col + 4 * i

        @pl.when(row == 3)
        def _():
            cur[...] = cot[chunk(c), :]

        @pl.when(row == 2)
        def _():
            arrived(gin.at[chunk(i), :], bwd_r.at[i])
            cur[...] = gin[chunk(i), :]

        def layer(back, carry):
            j = 3 - back
            cell = i * 4 + j
            rows = chunk(cell)
            grad = cur[...]
            og[rows, :] = grad
            pre_grad = (dot_nn(grad, w2[j]) * dg[rows, :]).astype(BF16)
            norm_grad = dot_nt(pre_grad, w1[j])
            one = unit[rows, :]
            inner = jnp.mean(norm_grad * one, axis=-1, keepdims=True)
            merged_grad = (grad.astype(F32) + scale[rows, :] * (norm_grad - one * inner)).astype(BF16)
            mg[rows, :] = merged_grad
            cur[...] = merged_grad

            @pl.when(j == 0)
            def _():
                remote(mg.at[rows, :], gin.at[chunk(i), :], bwd_s.at[i], bwd_r.at[i], sec - 4, dp).start()

            sg[rows, :] = dot_nt(merged_grad, ws[j]).astype(BF16)
            mirrored = i * 4 + (3 - j)
            remote(sg.at[rows, :], gskip.at[chunk(mirrored), :], gsk_s.at[cell], gsk_r.at[mirrored],
                   far_row * 4 + col, dp).start()
            give(3, og, cell, ogf, j, c)
            give(4, mg, cell, mgf, j, c)
            return carry

        lax.fori_loop(0, 4, layer, 0)

    def upper_again(c, carry):
        rows = chunk(c)

        @pl.when(lax.rem(c, 4) != col)
        def _():
            for kind, full in enumerate((out, mf, skf, ogf, mgf)):
                arrived(full.at[rows, :], own_r.at[kind, c])

        one = normalise(mf[rows, :].astype(F32))[1]
        norm = one.astype(BF16)
        pre = dot_nn(norm, w1[col]) + bias[col, pl.ds(micro(c), 1), :]
        square, t, gate = gelu_parts(pre)
        hid[rows, :] = (pre * gate).astype(BF16)
        normed[rows, :] = norm
        pg[rows, :] = (dot_nn(ogf[rows, :], w2[col]) * gelu_slope(pre, square, t, gate)).astype(BF16)
        return carry

    @pl.when(lower)
    def _():
        loads[3].wait()
        bias[col] = dot_nn(clk[...], wt[...])
        for which in (4, 0, 1):
            loads[which].wait()

        @pl.when(sec == 0)
        def _():
            for m in range(MICRO):
                xin[m * HEIGHT:(m + 1) * HEIGHT, :] = turned(lat[m])

        pl.semaphore_wait(barrier, greetings)

        @pl.when(row == 1)
        def _():
            gather(2, True, False)

        lax.fori_loop(0, N, lower_forward, 0)

        @pl.when(row == 0)
        def _():
            def later(c, carry):
                send_skip(c)
                return carry

            lax.fori_loop(0, N, later, 0)
            gather(2, True, False)

        for which in (2, 5):
            loads[which].wait()
        lax.fori_loop(0, N, hand_input, 0)
        gather(2, False, True)
        lax.fori_loop(0, N, lower_prepare, 0)
        lower_backward(0)
        lower_backward(1)
        lax.fori_loop(0, N, lower_again, 0)

    @pl.when(upper)
    def _():
        for which in (0, 1, 2):
            loads[which].wait()
        pl.semaphore_wait(barrier, greetings)
        gather(3, True, False)
        loads[3].wait()
        bias[col] = dot_nn(clk[...], wt[...])
        for which in (4, 5):
            loads[which].wait()
        gather(3, False, True)

        @pl.when(row == 3)
        def _():
            for m in range(MICRO):
                cot[m * HEIGHT:(m + 1) * HEIGHT, :] = turned(cot_t[m])

        def turn(s, carry):
            late = row == 3
            is_forward = jnp.where(late, lax.rem(s, 2) == 0, s < 2)
            i = jnp.where(late, lax.div(s, 2), lax.rem(s, 2))

            @pl.when(is_forward)
            def _():
                upper_forward(i)

            @pl.when(jnp.logical_not(is_forward))
            def _():
                upper_backward(i)

            return carry

        lax.fori_loop(0, 4, turn, 0)
        lax.fori_loop(0, N, upper_again, 0)

    item_a = Item(C, F // 2, True, 1, ga, (a_ps, a_pr, a_acc, a_zs, a_zr, a_cb),
                  (a_sp, a_rp, a_sz, a_rz, a_sg, a_rg, a_sf, a_rf))
    item_b = Item(C, F // 2, True, -1, gb, (b_ps, b_pr, b_acc, b_zs, b_zr, b_cb),
                  (b_sp, b_rp, b_sz, b_rz, b_sg, b_rg, b_sf, b_rf))
    item_c = Item(CPAD // 2, C, False, 1, gc, (c_ps, c_pr, c_acc, c_zs, c_zr, c_cb),
                  (c_sp, c_rp, c_sz, c_rz, c_sg, c_rg, c_sf, c_rf))

    def part_a(k):
        columns = pl.ds(pl.multiple_of(k * (F // 2), 128), F // 2)
        return dot_tn(ogf[...], hid[:, columns])

    def part_b(k):
        columns = pl.ds(pl.multiple_of(k * (F // 2), 128), F // 2)
        return dot_tn(normed[...], pg[:, columns])

    def part_c(k):
        return gcfull[pl.ds(pl.multiple_of(k * (CPAD // 2), 16), CPAD // 2), :]

    def pair_send(item):
        return remote(item.psend, item.precv, item.ps.at[0], item.pr.at[0], sec, partner)

    def pair_start(item, part):
        item.psend[...] = part(1 - core).astype(BF16)
        pair_send(item).start()

    def z_start(item, part):
        item.acc[...] = part(core)
        pair_send(item).wait_recv()
        total = item.acc[...] + item.precv[...].astype(F32)
        item.acc[...] = total
        item.zsend[...] = total.astype(BF16)
        hand = item.hand
        remote(item.zsend.at[item.rows(quarter_at[2]), :], item.zrecv.at[0],
               item.zs.at[0], item.zr.at[0], sec, device_at[hand]).start()
        remote(item.zsend.at[item.rows(quarter_at[-hand]), :], item.zrecv.at[1],
               item.zs.at[1], item.zr.at[1], sec, device_at[-hand]).start()

    def z_relay(item):
        hand = item.hand
        arrived(item.zrecv.at[0], item.zr.at[0])
        term = item.acc[item.rows(quarter_at[hand]), :] + item.zrecv[0].astype(F32)
        item.comb[...] = term.astype(BF16)
        remote(item.comb, item.zrecv.at[2], item.zs.at[2], item.zr.at[2], sec, device_at[hand]).start()

    def pass_on(item, d, n):
        spot = item.place(core, quarter_at[d])
        remote(spot, spot, item.fs.at[n], item.fr.at[n], sec, partner).start()

    def spread(item, d, n, to):
        spot = item.place(core, quarter_at[d])
        remote(spot, spot, item.gs.at[n], item.gr.at[n], sec, device_at[to]).start()

    def gather_start(item):
        arrived(item.zrecv.at[1], item.zr.at[1])
        arrived(item.zrecv.at[2], item.zr.at[2])
        total = item.acc[item.rows(zed), :] + item.zrecv[1].astype(F32) + item.zrecv[2].astype(F32)
        item.place(core, zed)[...] = total.astype(BF16)
        spread(item, 0, 0, item.hand)
        spread(item, 0, 1, -item.hand)
        pass_on(item, 0, 0)

    def near_pass(item):
        hand = item.hand
        arrived(item.place(core, quarter_at[-hand]), item.gr.at[0])
        spread(item, -hand, 2, hand)
        pass_on(item, -hand, 1)
        arrived(item.place(core, quarter_at[hand]), item.gr.at[1])
        pass_on(item, hand, 2)

    def far_pass(item):
        arrived(item.place(core, quarter_at[2]), item.gr.at[2])
        pass_on(item, 2, 3)

    def finish(item):
        for n, d in enumerate((0, -item.hand, item.hand, 2)):
            arrived(item.place(1 - core, quarter_at[d]), item.fr.at[n])
        pair_send(item).wait_send()
        quarter = item.zrecv.at[0]
        for n in range(3):
            sent(quarter, item.zs.at[n])
            sent(quarter, item.gs.at[n])
        for n in range(4):
            sent(quarter, item.fs.at[n])

    pair_start(item_a, part_a)
    pair_start(item_b, part_b)
    z_start(item_a, part_a)
    z_start(item_b, part_b)

    batch_of_row = lax.div(lax.broadcasted_iota(jnp.int32, (8, ROWS), 1), HEIGHT)
    batch_of_sum = lax.broadcasted_iota(jnp.int32, (8, ROWS), 0)
    chosen = jnp.where(batch_of_row == batch_of_sum, 1.0, 0.0).astype(BF16)
    sums = dot_nn(chosen, pg[...])
    z_relay(item_a)
    z_relay(item_b)
    trow[dp] = jnp.concatenate([sums, clk[...].astype(F32), jnp.zeros((8, WIDE - F - C), F32)], axis=1).astype(BF16)

    def time_move(d, n, replica):
        spot = trow.at[quarter_at[d] * 2 + core]
        return remote(spot, spot, t_s.at[n], t_r.at[n], sec, replica)

    offsets = (1, -1, 2)
    for n, d in enumerate(offsets):
        time_move(0, n, device_at[d]).start()
    time_move(0, 3, partner).start()

    @pl.when(upper)
    def _():
        gcfull[...] = jnp.zeros_like(gcfull)
        gcfull[0:C, :] = dot_tn(skf[...], mgf[...])
        pair_start(item_c, part_c)
        z_start(item_c, part_c)
        z_relay(item_c)

    gather_start(item_a)
    gather_start(item_b)

    for n, d in enumerate(offsets):
        source = -d if d != 2 else 2
        arrived(trow.at[quarter_at[source] * 2 + core], t_r.at[n])
        time_move(source, 4 + n, partner).start()

    near_pass(item_a)
    near_pass(item_b)

    @pl.when(upper)
    def _():
        gather_start(item_c)
        near_pass(item_c)

    for m in range(MICRO):
        out_t[m] = turned(out[m * HEIGHT:(m + 1) * HEIGHT, :])

    far_pass(item_a)
    far_pass(item_b)

    @pl.when(upper)
    def _():
        far_pass(item_c)
        finish(item_c)

    @pl.when(lower)
    def _():
        gc[...] = jnp.zeros_like(gc)

    for n in range(7):
        d = 0 if n < 4 else (-1, 1, 2)[n - 4]
        if n >= 3:
            arrived(trow.at[quarter_at[d] * 2 + (1 - core)], t_r.at[n])
        sent(trow.at[dp], t_s.at[n])

    some = xin.at[chunk(0), :]

    @pl.when(lower)
    def _():
        def drain(c, carry):
            sent(some, fwd_s.at[c])

            @pl.when(sec < HALF - 1)
            def _():
                sent(some, skip_s.at[c])

            @pl.when(lax.rem(c, 4) != col)
            def _():
                sent(some, in_s.at[c])
                sent(some, own_s.at[3, c])

            return carry

        lax.fori_loop(0, N, drain, 0)

        @pl.when(row == 1)
        def _():
            for i in range(2):
                sent(some, bwd_s.at[i])

    @pl.when(upper)
    def _():
        def drain(cell, carry):
            sent(some, gsk_s.at[cell])

            @pl.when(lax.rem(cell, 4) != col)
            def _():
                for kind in range(5):
                    sent(some, own_s.at[kind, cell])

            return carry

        lax.fori_loop(0, N, drain, 0)
        for i in range(2):
            sent(some, bwd_s.at[i])

            @pl.when(row == 2)
            def _():
                sent(some, fwd_s.at[i])

    finish(item_a)
    finish(item_b)


def finishing(ga, gb, gc, trow, out_t, a_out, b_out, t_out, s_out, o_out, clock_t):
    upper = lax.axis_index("section") >= HALF
    block = pl.program_id(0)

    @pl.when(block == 0)
    def _():
        clock_t[...] = jnp.transpose(trow[:, F:F + C].astype(F32)).astype(BF16)

    rows = pl.ds(pl.multiple_of(block * BLOCK, BLOCK), BLOCK)
    a_out[...] = ga[...].astype(F32)
    b_out[...] = gb[...].astype(F32)
    t_out[...] = dot_nn(clock_t[rows, :], trow[:, 0:F])
    s_out[...] = jnp.where(upper, gc[...].astype(F32), 0.0)
    o_out[...] = out_t[...]


def item_scratch(rows, cols):
    return [
        pltpu.VMEM((rows, cols), BF16),
        pltpu.VMEM((rows, cols), BF16),
        pltpu.VMEM((rows, cols), F32),
        pltpu.VMEM((rows, cols), BF16),
        pltpu.VMEM((Z - 1, rows // Z, cols), BF16),
        pltpu.VMEM((rows // Z, cols), BF16),
    ]


def item_sems():
    counts = (1, 1, 3, 3, 3, 3, 4, 4)
    return [pltpu.SemaphoreType.DMA((count,)) for count in counts]


def local(latents, steps, cotangent, w_in, w_out, w_time, w_skip):
    vmem = pl.BlockSpec(memory_space=pltpu.VMEM)
    anywhere = pl.BlockSpec(memory_space=pl.ANY)
    rows_c = pltpu.VMEM((ROWS, C), BF16)
    rows_f = pltpu.VMEM((ROWS, F), BF16)
    dma = pltpu.SemaphoreType.DMA
    out_t, ga, gb, gc, trow = pl.pallas_call(
        kernel,
        out_shape=(
            jax.ShapeDtypeStruct((MICRO, C, HEIGHT), BF16),
            jax.ShapeDtypeStruct((C, F), BF16),
            jax.ShapeDtypeStruct((C, F), BF16),
            jax.ShapeDtypeStruct((CPAD, C), BF16),
            jax.ShapeDtypeStruct((DP, 8, WIDE), BF16),
        ),
        in_specs=[anywhere, pl.BlockSpec(memory_space=pltpu.SMEM)] + [anywhere] * 5,
        out_specs=(vmem,) * 5,
        scratch_shapes=[
            pltpu.VMEM((MICRO, C, HEIGHT), BF16),
            pltpu.VMEM((MICRO, C, HEIGHT), BF16),
            rows_c,
            pltpu.VMEM((4, C, F), BF16),
            pltpu.VMEM((4, C, F), BF16),
            pltpu.VMEM((4, C, C), BF16),
            pltpu.VMEM((C, F), BF16),
            pltpu.VMEM((4, 8, F), F32),
            pltpu.VMEM((8, C), BF16),
            rows_c, rows_c, rows_c, rows_c,
            rows_c, rows_c,
            pltpu.VMEM((ROWS, C), F32),
            pltpu.VMEM((ROWS, 1), F32),
            pltpu.VMEM((ROWS, F), F32),
            pltpu.VMEM((ROWS, F), F32),
            rows_c, rows_c, rows_c,
            pltpu.VMEM((R, C), BF16),
            rows_c, rows_c, rows_c, rows_c, rows_c, rows_c,
            rows_f, rows_f,
            pltpu.VMEM((CPAD, C), F32),
        ]
        + item_scratch(C, F // 2)
        + item_scratch(C, F // 2)
        + item_scratch(CPAD // 2, C)
        + [dma((6,))]
        + [dma((N,))] * 8
        + [dma((5, N))] * 2
        + [dma((N,))] * 2
        + [dma((3, 12))] * 2
        + [dma((3,))] * 2
        + item_sems() + item_sems() + item_sems()
        + [dma((DP - 1,))] * 2,
        compiler_params=pltpu.CompilerParams(
            collective_id=0, has_side_effects=True, vmem_limit_bytes=60 * 1024 * 1024
        ),
        name="relay",
    )(
        jnp.swapaxes(latents, 1, 2), steps, jnp.swapaxes(cotangent, 1, 2),
        w_in[0], jnp.swapaxes(w_out[0], 0, 1), w_time[0], w_skip[0],
    )
    wide = pl.BlockSpec((BLOCK, F), lambda i: (i, 0))
    narrow = pl.BlockSpec((BLOCK, C), lambda i: (i, 0))
    turned_rows = pl.BlockSpec((MICRO, BLOCK, HEIGHT), lambda i: (0, i, 0))
    grad_out_t, grad_in, grad_time, grad_skip, out_t = pl.pallas_call(
        finishing,
        grid=(C // BLOCK,),
        out_shape=(
            jax.ShapeDtypeStruct((C, F), F32),
            jax.ShapeDtypeStruct((C, F), F32),
            jax.ShapeDtypeStruct((C, F), F32),
            jax.ShapeDtypeStruct((C, C), F32),
            jax.ShapeDtypeStruct((MICRO, C, HEIGHT), BF16),
        ),
        in_specs=[wide, wide, narrow, pl.BlockSpec((DP * 8, WIDE), lambda i: (0, 0)), turned_rows],
        out_specs=(wide, wide, wide, narrow, turned_rows),
        scratch_shapes=[pltpu.VMEM((C, DP * 8), BF16)],
        name="finishing",
    )(ga, gb, gc, trow.reshape(DP * 8, WIDE), out_t)
    return (
        jnp.swapaxes(out_t, 1, 2)[None],
        grad_in[None], jnp.swapaxes(grad_out_t, 0, 1)[None], grad_time[None], grad_skip[None],
    )


def solution(mesh):
    placed = (
        P(None, "dp", None),
        P("dp", None),
        P(None, "dp", None),
        P("section", None, None),
        P("section", None, None),
        P("section", None, None),
        P("section", None, None),
    )
    return jax.shard_map(
        local,
        mesh=mesh,
        in_specs=placed,
        out_specs=(
            P("section", None, "dp", None),
            P("section", None, None),
            P("section", None, None),
            P("section", None, None),
            P("section", None, None),
        ),
        check_vma=False,
    )
```

```python
import math

import jax
import jax.numpy as jnp
from jax import lax
from jax.experimental import pallas as pl
from jax.experimental.pallas import tpu as pltpu
from jax.sharding import PartitionSpec as P

MESH = pl.DeviceIdType.MESH
F32 = jnp.float32
BF16 = jnp.bfloat16

SECTIONS = 16
HALF = 8
DP = 8
Z = 4
C = 320
F = 1280
MICRO = 4
HEIGHT = 128
ROWS = MICRO * HEIGHT
R = 64
N = ROWS // R
PER = HEIGHT // R
WIDE = 1664
CPAD = 384
BLOCK = 160
WIDTHS = (256, 384)
GELU_C = math.sqrt(2.0 / math.pi)


def dot_nn(a, b):
    return lax.dot_general(a, b, (((1,), (0,)), ((), ())), preferred_element_type=F32)


def dot_nt(a, b):
    return lax.dot_general(a, b, (((1,), (1,)), ((), ())), preferred_element_type=F32)


def dot_tn(a, b):
    return lax.dot_general(a, b, (((0,), (0,)), ((), ())), preferred_element_type=F32)


class Item:
    def __init__(self, half_rows, half_cols, by_cols, hand, out, refs, sems, offset=0):
        self.half_rows = half_rows
        self.half_cols = half_cols
        self.by_cols = by_cols
        self.hand = hand
        self.offset = offset
        self.quarter = half_rows // Z
        self.out = out
        self.psend, self.precv, self.acc, self.zsend, self.zrecv, self.comb = refs
        (self.ps, self.pr, self.zs, self.zr, self.gs, self.gr, self.fs, self.fr) = sems

    def place(self, core, z):
        if self.by_cols:
            return self.out.at[
                pl.ds(pl.multiple_of(z * self.quarter, 16), self.quarter),
                pl.ds(pl.multiple_of(core * (F // 2) + self.offset, 128), self.half_cols),
            ]
        start = pl.multiple_of(core * self.half_rows + z * self.quarter, 16)
        return self.out.at[pl.ds(start, self.quarter), :]

    def rows(self, z):
        return pl.ds(pl.multiple_of(z * self.quarter, 16), self.quarter)


def gelu_parts(pre):
    square = pre * pre
    t = jnp.tanh(pre * (GELU_C + (GELU_C * 0.044715) * square))
    gate = 0.5 + 0.5 * t
    return square, t, gate


def gelu_slope(pre, square, t, gate):
    return gate + (0.5 * pre) * (1.0 - t * t) * (GELU_C + (3.0 * GELU_C * 0.044715) * square)


def normalise(wide):
    factor = lax.rsqrt(jnp.mean(wide * wide, axis=-1, keepdims=True) + 1e-05)
    return factor, wide * factor


def turned(block):
    return jnp.transpose(block.astype(F32)).astype(BF16)


def kernel(
    lat_h, steps, cot_h, w1_h, w2_h, wt_h, ws_h,
    out_t, ga, gb, gc, trow,
    lat, cot_t, cot, w1, w2, ws, wt, bias, clk,
    xin, skip, gin, gskip, obuf, merged, unit, scale, dg, dgo, og, mg, sg, cur,
    out, mf, skf, ogf, mgf, normed, hid, pg, gcfull,
    *rest,
):
    pieces, rest = rest[:5 * 6], rest[5 * 6:]
    (load, fwd_s, fwd_r, skip_s, skip_r, bwd_s, bwd_r, gsk_s, gsk_r,
     own_s, own_r, in_s, in_r, gw_s, gw_r, bias_s, bias_r) = rest[:17]
    sems, (t_s, t_r) = rest[17:-2], rest[-2:]
    sec = lax.axis_index("section")
    dp = lax.axis_index("dp")
    core = lax.rem(dp, 2)
    zed = lax.div(dp, 2)
    row = lax.div(sec, 4)
    col = lax.rem(sec, 4)
    far_row = 3 - row
    upper = sec >= HALF
    lower = sec < HALF
    own = col
    partner = zed * 2 + (1 - core)
    quarter_at = {d: lax.rem(zed + d + Z, Z) for d in (-1, 0, 1, 2)}
    device_at = {d: quarter_at[d] * 2 + core for d in (-1, 1, 2)}

    loads = [
        pltpu.make_async_copy(w1_h, w1.at[own], load.at[0]),
        pltpu.make_async_copy(w2_h, w2.at[own], load.at[1]),
        pltpu.make_async_copy(ws_h, ws.at[own], load.at[2]),
        pltpu.make_async_copy(wt_h, wt, load.at[3]),
        pltpu.make_async_copy(lat_h, lat, load.at[4]),
        pltpu.make_async_copy(cot_h, cot_t, load.at[5]),
    ]
    for which in (3, 4, 0, 1, 2, 5):
        loads[which].start()

    barrier = pltpu.get_barrier_semaphore()

    def greet(section, replica):
        pl.semaphore_signal(barrier, inc=1, device_id=(section, replica), device_id_type=MESH)

    for k in range(1, DP):
        greet(sec, lax.rem(dp + k, DP))
    for k in range(4):
        greet(far_row * 4 + k, dp)

    for k in range(1, 4):
        greet(row * 4 + lax.rem(col + k, 4), dp)
    greet((row + 1 - 2 * lax.rem(row, 2)) * 4 + col, dp)
    bend = (sec == 3) | (sec == 4)

    @pl.when(bend)
    def _():
        greet(7 - sec, dp)

    greetings = jnp.where(bend, 16, 15)

    def remote(src, dst, ssem, rsem, section, replica):
        return pltpu.make_async_remote_copy(
            src_ref=src, dst_ref=dst, send_sem=ssem, recv_sem=rsem,
            device_id=(section, replica), device_id_type=MESH,
        )

    def arrived(spot, rsem):
        remote(spot, spot, rsem, rsem, sec, partner).wait_recv()

    def sent(spot, ssem):
        remote(spot, spot, ssem, ssem, sec, partner).wait_send()

    batch = lax.broadcasted_iota(jnp.int32, (8, C // 2), 0)
    step = jnp.zeros((8, C // 2), F32)
    for m in range(MICRO):
        step = jnp.where(batch == m, steps[0, m].astype(F32), step)
    place = lax.broadcasted_iota(jnp.int32, (8, C // 2), 1).astype(F32)
    angle = step * jnp.exp(-math.log(10000.0) * place / (C // 2))
    real = batch < MICRO
    clk[:, 0:C // 2] = jnp.where(real, jnp.sin(angle), 0.0).astype(BF16)
    clk[:, C // 2:C] = jnp.where(real, jnp.cos(angle), 0.0).astype(BF16)
    def chunk(c):
        return pl.ds(pl.multiple_of(c * R, R), R)

    def micro(c):
        return lax.div(c, PER)

    def send_skip(c):
        cell = lax.div(c, 4) * 4 + (3 - col)
        remote(out.at[chunk(c), :], skip.at[chunk(cell), :], skip_s.at[c], skip_r.at[cell],
               far_row * 4 + lax.rem(c, 4), dp).start()

    def lower_forward(c, carry):
        rows = chunk(c)

        @pl.when(sec > 0)
        def _():
            arrived(xin.at[rows, :], fwd_r.at[c])

        wide = xin[rows, :].astype(F32)
        norm = normalise(wide)[1].astype(BF16)
        pre = dot_nn(norm, w1[col]) + bias[col, pl.ds(micro(c), 1), :]
        square, t, gate = gelu_parts(pre)
        hidden = (pre * gate).astype(BF16)
        out[rows, :] = (wide + dot_nt(hidden, w2[col])).astype(BF16)

        @pl.when(sec < HALF - 1)
        def _():
            remote(out.at[rows, :], xin.at[rows, :], fwd_s.at[c], fwd_r.at[c], sec + 1, dp).start()

        @pl.when((row == 1) & (sec < HALF - 1))
        def _():
            send_skip(c)

        @pl.when(sec == HALF - 1)
        def _():
            i = lax.div(c, 4)
            remote(out.at[rows, :], xin.at[chunk(i), :], fwd_s.at[c], fwd_r.at[i],
                   HALF + lax.rem(c, 4), dp).start()

        hid[rows, :] = hidden
        normed[rows, :] = norm
        dgo[rows, :] = gelu_slope(pre, square, t, gate)
        return carry

    def hand_input(c, carry):
        cell = lax.div(c, 4) * 4 + col
        place_of = lax.rem(c, 4)

        @pl.when(place_of == col)
        def _():
            merged[chunk(cell), :] = xin[chunk(c), :]

        @pl.when(place_of != col)
        def _():
            remote(xin.at[chunk(c), :], merged.at[chunk(cell), :], in_s.at[c], in_r.at[cell],
                   row * 4 + place_of, dp).start()

        return carry

    def lower_prepare(cell, carry):
        j = lax.rem(cell, 4)
        c = col + 4 * lax.div(cell, 4)
        rows = chunk(cell)

        @pl.when(j != col)
        def _():
            arrived(merged.at[rows, :], in_r.at[cell])

        factor, one = normalise(merged[rows, :].astype(F32))
        pre = dot_nn(one.astype(BF16), w1[j]) + bias[j, pl.ds(micro(c), 1), :]
        square, t, gate = gelu_parts(pre)
        unit[rows, :] = one
        scale[rows, :] = factor
        dg[rows, :] = gelu_slope(pre, square, t, gate)
        return carry

    def lower_backward(i):
        c = col + 4 * i
        arrived(gin.at[chunk(i), :], bwd_r.at[i])
        cur[...] = gin[chunk(i), :]

        def layer(back, carry):
            j = 3 - back
            cell = i * 4 + j
            rows = chunk(cell)
            arrived(gskip.at[rows, :], gsk_r.at[cell])
            grad = (cur[...].astype(F32) + gskip[rows, :].astype(F32)).astype(BF16)
            og[rows, :] = grad
            give(3, og, cell, ogf, j, c)
            pre_grad = (dot_nn(grad, w2[j]) * dg[rows, :]).astype(BF16)
            norm_grad = dot_nt(pre_grad, w1[j])
            one = unit[rows, :]
            inner = jnp.mean(norm_grad * one, axis=-1, keepdims=True)
            merged_grad = (grad.astype(F32) + scale[rows, :] * (norm_grad - one * inner)).astype(BF16)
            cur[...] = merged_grad

            @pl.when((row == 1) & (j == 0))
            def _():
                mg[rows, :] = merged_grad
                remote(mg.at[rows, :], gin.at[chunk(i), :], bwd_s.at[i], bwd_r.at[i], sec - 4, dp).start()

            return carry

        lax.fori_loop(0, 4, layer, 0)

    def lower_again(c, carry):
        rows = chunk(c)

        @pl.when(lax.rem(c, 4) != col)
        def _():
            arrived(ogf.at[rows, :], own_r.at[3, c])

        pg[rows, :] = (dot_nn(ogf[rows, :], w2[col]) * dgo[rows, :]).astype(BF16)
        return carry

    def gather(count, opening, closing):
        arrays = ((w1, C // 4), (w2, C // 4), (ws, C // 4))
        to_right = row * 4 + lax.rem(col + 1, 4)
        to_left = row * 4 + lax.rem(col + 3, 4)
        left, right, far = lax.rem(col + 3, 4), lax.rem(col + 1, 4), lax.rem(col + 2, 4)

        def piece(which, slot, half, q):
            size = arrays[which][1]
            start = pl.multiple_of(half * (2 * size) + q * size, 16)
            return arrays[which][0].at[slot, pl.ds(start, size), :]

        def move(which, slot, half, q, n, section, replica):
            spot = piece(which, slot, half, q)
            return remote(spot, spot, gw_s.at[which, n], gw_r.at[which, n], section, replica)

        passed = ((left, 0), (left, 1), (right, 0), (right, 1), (far, 0), (far, 1))

        def forward_on(which, n):
            slot, q = passed[n]
            move(which, slot, core, q, 6 + n, sec, partner).start()

        def got(which, n):
            slot, q = passed[n]
            arrived(piece(which, slot, core, q), gw_r.at[which, n])

        if opening:
            for which in range(count):
                move(which, col, core, 0, 0, to_right, dp).start()
                move(which, col, core, 1, 3, to_left, dp).start()
                move(which, col, core, 1, 1, to_right, dp).start()
                move(which, col, core, 0, 2, to_left, dp).start()
        if not closing:
            return
        for k in range(1, 4):
            remote(bias.at[col], bias.at[col], bias_s.at[k - 1], bias_r.at[k - 1],
                   row * 4 + lax.rem(col + k, 4), dp).start()
        for which in range(count):
            got(which, 0)
            move(which, left, core, 0, 4, to_right, dp).start()
            forward_on(which, 0)
            got(which, 3)
            move(which, right, core, 1, 5, to_left, dp).start()
            forward_on(which, 3)
            for n in (1, 2):
                got(which, n)
                forward_on(which, n)
        for which in range(count):
            for n in (4, 5):
                got(which, n)
                forward_on(which, n)
        for which in range(count):
            for n in range(6):
                slot, q = passed[n]
                arrived(piece(which, slot, 1 - core, q), gw_r.at[which, 6 + n])
        for k in range(1, 4):
            arrived(bias.at[lax.rem(col + 4 - k, 4)], bias_r.at[k - 1])
        for which in range(count):
            for n in range(12):
                sent(piece(which, col, core, 0), gw_s.at[which, n])
        for k in range(3):
            sent(bias.at[col], bias_s.at[k])

    def give(kind, buffer, cell, full, j, c):
        @pl.when(j == col)
        def _():
            full[chunk(c), :] = buffer[chunk(cell), :]

        @pl.when(j != col)
        def _():
            remote(buffer.at[chunk(cell), :], full.at[chunk(c), :], own_s.at[kind, cell],
                   own_r.at[kind, c], row * 4 + j, dp).start()

    def upper_forward(i):
        c = col + 4 * i
        arrived(xin.at[chunk(i), :], fwd_r.at[i])
        cur[...] = xin[chunk(i), :]

        def layer(j, carry):
            cell = i * 4 + j
            rows = chunk(cell)
            first = (row == 2) & (j == 0)

            @pl.when(first)
            def _():
                skip[rows, :] = cur[...]

            @pl.when(jnp.logical_not(first))
            def _():
                arrived(skip.at[rows, :], skip_r.at[cell])

            total = cur[...].astype(F32) + dot_nn(skip[rows, :], ws[j])
            joined = total.astype(BF16)
            wide = joined.astype(F32)
            factor, one = normalise(wide)
            pre = dot_nn(one.astype(BF16), w1[j]) + bias[j, pl.ds(micro(c), 1), :]
            square, t, gate = gelu_parts(pre)
            hidden = (pre * gate).astype(BF16)
            result = (wide + dot_nt(hidden, w2[j])).astype(BF16)
            obuf[rows, :] = result
            cur[...] = result

            @pl.when((row == 2) & (j == 3))
            def _():
                remote(obuf.at[rows, :], xin.at[chunk(i), :], fwd_s.at[i], fwd_r.at[i], sec + 4, dp).start()

            merged[rows, :] = joined
            unit[rows, :] = one
            scale[rows, :] = factor
            dg[rows, :] = gelu_slope(pre, square, t, gate)
            give(0, obuf, cell, out, j, c)
            give(1, merged, cell, mf, j, c)
            give(2, skip, cell, skf, j, c)
            return carry

        lax.fori_loop(0, 4, layer, 0)

    def upper_backward(i):
        c = col + 4 * i

        @pl.when(row == 3)
        def _():
            cur[...] = cot[chunk(c), :]

        @pl.when(row == 2)
        def _():
            arrived(gin.at[chunk(i), :], bwd_r.at[i])
            cur[...] = gin[chunk(i), :]

        def layer(back, carry):
            j = 3 - back
            cell = i * 4 + j
            rows = chunk(cell)
            grad = cur[...]
            og[rows, :] = grad
            pre_grad = (dot_nn(grad, w2[j]) * dg[rows, :]).astype(BF16)
            norm_grad = dot_nt(pre_grad, w1[j])
            one = unit[rows, :]
            inner = jnp.mean(norm_grad * one, axis=-1, keepdims=True)
            merged_grad = (grad.astype(F32) + scale[rows, :] * (norm_grad - one * inner)).astype(BF16)
            mg[rows, :] = merged_grad
            cur[...] = merged_grad

            @pl.when(j == 0)
            def _():
                remote(mg.at[rows, :], gin.at[chunk(i), :], bwd_s.at[i], bwd_r.at[i], sec - 4, dp).start()

            sg[rows, :] = dot_nt(merged_grad, ws[j]).astype(BF16)
            mirrored = i * 4 + (3 - j)
            remote(sg.at[rows, :], gskip.at[chunk(mirrored), :], gsk_s.at[cell], gsk_r.at[mirrored],
                   far_row * 4 + col, dp).start()
            give(3, og, cell, ogf, j, c)
            give(4, mg, cell, mgf, j, c)
            return carry

        lax.fori_loop(0, 4, layer, 0)

    def upper_again(c, carry):
        rows = chunk(c)

        @pl.when(lax.rem(c, 4) != col)
        def _():
            for kind, full in enumerate((out, mf, skf, ogf, mgf)):
                arrived(full.at[rows, :], own_r.at[kind, c])

        one = normalise(mf[rows, :].astype(F32))[1]
        norm = one.astype(BF16)
        pre = dot_nn(norm, w1[col]) + bias[col, pl.ds(micro(c), 1), :]
        square, t, gate = gelu_parts(pre)
        hid[rows, :] = (pre * gate).astype(BF16)
        normed[rows, :] = norm
        pg[rows, :] = (dot_nn(ogf[rows, :], w2[col]) * gelu_slope(pre, square, t, gate)).astype(BF16)
        return carry

    @pl.when(lower)
    def _():
        loads[3].wait()
        bias[col] = dot_nn(clk[...], wt[...])
        for which in (4, 0, 1):
            loads[which].wait()

        @pl.when(sec == 0)
        def _():
            for m in range(MICRO):
                xin[m * HEIGHT:(m + 1) * HEIGHT, :] = turned(lat[m])

        pl.semaphore_wait(barrier, greetings)

        @pl.when(row == 1)
        def _():
            gather(2, True, False)

        lax.fori_loop(0, N, lower_forward, 0)

        @pl.when(row == 0)
        def _():
            def later(c, carry):
                send_skip(c)
                return carry

            lax.fori_loop(0, N, later, 0)
            gather(2, True, False)

        for which in (2, 5):
            loads[which].wait()
        lax.fori_loop(0, N, hand_input, 0)
        gather(2, False, True)
        lax.fori_loop(0, N, lower_prepare, 0)
        lower_backward(0)
        lower_backward(1)
        lax.fori_loop(0, N, lower_again, 0)

    @pl.when(upper)
    def _():
        for which in (0, 1, 2):
            loads[which].wait()
        pl.semaphore_wait(barrier, greetings)
        gather(3, True, False)
        loads[3].wait()
        bias[col] = dot_nn(clk[...], wt[...])
        for which in (4, 5):
            loads[which].wait()
        gather(3, False, True)

        @pl.when(row == 3)
        def _():
            for m in range(MICRO):
                cot[m * HEIGHT:(m + 1) * HEIGHT, :] = turned(cot_t[m])

        def turn(s, carry):
            late = row == 3
            is_forward = jnp.where(late, lax.rem(s, 2) == 0, s < 2)
            i = jnp.where(late, lax.div(s, 2), lax.rem(s, 2))

            @pl.when(is_forward)
            def _():
                upper_forward(i)

            @pl.when(jnp.logical_not(is_forward))
            def _():
                upper_backward(i)

            return carry

        lax.fori_loop(0, 4, turn, 0)
        lax.fori_loop(0, N, upper_again, 0)

    def columns(k, offset, width):
        return pl.ds(pl.multiple_of(k * (F // 2) + offset, 128), width)

    def grad_item(n, hand, into, left, right, offset, width):
        item = Item(C, width, True, hand, into, pieces[6 * n:6 * n + 6], sems[8 * n:8 * n + 8], offset)
        item.part = lambda k: dot_tn(left[...], right[:, columns(k, offset, width)])
        return item

    items = [
        grad_item(0, 1, ga, ogf, hid, 0, WIDTHS[0]),
        grad_item(1, -1, gb, normed, pg, 0, WIDTHS[0]),
        grad_item(2, 1, ga, ogf, hid, WIDTHS[0], WIDTHS[1]),
        grad_item(3, -1, gb, normed, pg, WIDTHS[0], WIDTHS[1]),
    ]
    item_c = Item(CPAD // 2, C, False, 1, gc, pieces[24:30], sems[32:40])
    item_c.part = lambda k: gcfull[pl.ds(pl.multiple_of(k * (CPAD // 2), 16), CPAD // 2), :]

    def pair_send(item):
        return remote(item.psend, item.precv, item.ps.at[0], item.pr.at[0], sec, partner)

    def pair_start(item):
        item.psend[...] = item.part(1 - core).astype(BF16)
        pair_send(item).start()

    def z_start(item):
        item.acc[...] = item.part(core)
        pair_send(item).wait_recv()
        total = item.acc[...] + item.precv[...].astype(F32)
        item.acc[...] = total
        item.zsend[...] = total.astype(BF16)
        hand = item.hand
        remote(item.zsend.at[item.rows(quarter_at[2]), :], item.zrecv.at[0],
               item.zs.at[0], item.zr.at[0], sec, device_at[hand]).start()
        remote(item.zsend.at[item.rows(quarter_at[-hand]), :], item.zrecv.at[1],
               item.zs.at[1], item.zr.at[1], sec, device_at[-hand]).start()

    def z_relay(item):
        hand = item.hand
        arrived(item.zrecv.at[0], item.zr.at[0])
        term = item.acc[item.rows(quarter_at[hand]), :] + item.zrecv[0].astype(F32)
        item.comb[...] = term.astype(BF16)
        remote(item.comb, item.zrecv.at[2], item.zs.at[2], item.zr.at[2], sec, device_at[hand]).start()

    def pass_on(item, d, n):
        spot = item.place(core, quarter_at[d])
        remote(spot, spot, item.fs.at[n], item.fr.at[n], sec, partner).start()

    def spread(item, d, n, to):
        spot = item.place(core, quarter_at[d])
        remote(spot, spot, item.gs.at[n], item.gr.at[n], sec, device_at[to]).start()

    def gather_start(item):
        arrived(item.zrecv.at[1], item.zr.at[1])
        arrived(item.zrecv.at[2], item.zr.at[2])
        total = item.acc[item.rows(zed), :] + item.zrecv[1].astype(F32) + item.zrecv[2].astype(F32)
        item.place(core, zed)[...] = total.astype(BF16)
        spread(item, 0, 0, item.hand)
        spread(item, 0, 1, -item.hand)
        pass_on(item, 0, 0)

    def near_pass(item):
        hand = item.hand
        arrived(item.place(core, quarter_at[-hand]), item.gr.at[0])
        spread(item, -hand, 2, hand)
        pass_on(item, -hand, 1)
        arrived(item.place(core, quarter_at[hand]), item.gr.at[1])
        pass_on(item, hand, 2)

    def far_pass(item):
        arrived(item.place(core, quarter_at[2]), item.gr.at[2])
        pass_on(item, 2, 3)

    def finish(item):
        for n, d in enumerate((0, -item.hand, item.hand, 2)):
            arrived(item.place(1 - core, quarter_at[d]), item.fr.at[n])
        pair_send(item).wait_send()
        quarter = item.zrecv.at[0]
        for n in range(3):
            sent(quarter, item.zs.at[n])
            sent(quarter, item.gs.at[n])
        for n in range(4):
            sent(quarter, item.fs.at[n])

    for item in items:
        pair_start(item)
    for item in items:
        z_start(item)

    batch_of_row = lax.div(lax.broadcasted_iota(jnp.int32, (8, ROWS), 1), HEIGHT)
    batch_of_sum = lax.broadcasted_iota(jnp.int32, (8, ROWS), 0)
    chosen = jnp.where(batch_of_row == batch_of_sum, 1.0, 0.0).astype(BF16)
    sums = dot_nn(chosen, pg[...])
    for item in items:
        z_relay(item)
    trow[dp] = jnp.concatenate([sums, clk[...].astype(F32), jnp.zeros((8, WIDE - F - C), F32)], axis=1).astype(BF16)

    def time_move(d, n, replica):
        spot = trow.at[quarter_at[d] * 2 + core]
        return remote(spot, spot, t_s.at[n], t_r.at[n], sec, replica)

    offsets = (1, -1, 2)
    for n, d in enumerate(offsets):
        time_move(0, n, device_at[d]).start()
    time_move(0, 3, partner).start()

    @pl.when(upper)
    def _():
        gcfull[...] = jnp.zeros_like(gcfull)
        gcfull[0:C, :] = dot_tn(skf[...], mgf[...])
        pair_start(item_c)
        z_start(item_c)
        z_relay(item_c)

    for item in items:
        gather_start(item)

    for n, d in enumerate(offsets):
        source = -d if d != 2 else 2
        arrived(trow.at[quarter_at[source] * 2 + core], t_r.at[n])
        time_move(source, 4 + n, partner).start()

    for item in items:
        near_pass(item)

    @pl.when(upper)
    def _():
        gather_start(item_c)
        near_pass(item_c)

    for m in range(MICRO):
        out_t[m] = turned(out[m * HEIGHT:(m + 1) * HEIGHT, :])

    for item in items:
        far_pass(item)

    @pl.when(upper)
    def _():
        far_pass(item_c)
        finish(item_c)

    @pl.when(lower)
    def _():
        gc[...] = jnp.zeros_like(gc)

    for n in range(7):
        d = 0 if n < 4 else (-1, 1, 2)[n - 4]
        if n >= 3:
            arrived(trow.at[quarter_at[d] * 2 + (1 - core)], t_r.at[n])
        sent(trow.at[dp], t_s.at[n])

    some = xin.at[chunk(0), :]

    @pl.when(lower)
    def _():
        def drain(c, carry):
            sent(some, fwd_s.at[c])

            @pl.when(sec < HALF - 1)
            def _():
                sent(some, skip_s.at[c])

            @pl.when(lax.rem(c, 4) != col)
            def _():
                sent(some, in_s.at[c])
                sent(some, own_s.at[3, c])

            return carry

        lax.fori_loop(0, N, drain, 0)

        @pl.when(row == 1)
        def _():
            for i in range(2):
                sent(some, bwd_s.at[i])

    @pl.when(upper)
    def _():
        def drain(cell, carry):
            sent(some, gsk_s.at[cell])

            @pl.when(lax.rem(cell, 4) != col)
            def _():
                for kind in range(5):
                    sent(some, own_s.at[kind, cell])

            return carry

        lax.fori_loop(0, N, drain, 0)
        for i in range(2):
            sent(some, bwd_s.at[i])

            @pl.when(row == 2)
            def _():
                sent(some, fwd_s.at[i])

    for item in items:
        finish(item)


def finishing(ga, gb, gc, trow, out_t, a_out, b_out, t_out, s_out, o_out, clock_t):
    upper = lax.axis_index("section") >= HALF
    block = pl.program_id(0)

    @pl.when(block == 0)
    def _():
        clock_t[...] = jnp.transpose(trow[:, F:F + C].astype(F32)).astype(BF16)

    rows = pl.ds(pl.multiple_of(block * BLOCK, BLOCK), BLOCK)
    a_out[...] = ga[...].astype(F32)
    b_out[...] = gb[...].astype(F32)
    t_out[...] = dot_nn(clock_t[rows, :], trow[:, 0:F])
    s_out[...] = jnp.where(upper, gc[...].astype(F32), 0.0)
    o_out[...] = out_t[...]


def item_scratch(rows, cols):
    return [
        pltpu.VMEM((rows, cols), BF16),
        pltpu.VMEM((rows, cols), BF16),
        pltpu.VMEM((rows, cols), F32),
        pltpu.VMEM((rows, cols), BF16),
        pltpu.VMEM((Z - 1, rows // Z, cols), BF16),
        pltpu.VMEM((rows // Z, cols), BF16),
    ]


def item_sems():
    counts = (1, 1, 3, 3, 3, 3, 4, 4)
    return [pltpu.SemaphoreType.DMA((count,)) for count in counts]


def local(latents, steps, cotangent, w_in, w_out, w_time, w_skip):
    vmem = pl.BlockSpec(memory_space=pltpu.VMEM)
    anywhere = pl.BlockSpec(memory_space=pl.ANY)
    rows_c = pltpu.VMEM((ROWS, C), BF16)
    rows_f = pltpu.VMEM((ROWS, F), BF16)
    dma = pltpu.SemaphoreType.DMA
    out_t, ga, gb, gc, trow = pl.pallas_call(
        kernel,
        out_shape=(
            jax.ShapeDtypeStruct((MICRO, C, HEIGHT), BF16),
            jax.ShapeDtypeStruct((C, F), BF16),
            jax.ShapeDtypeStruct((C, F), BF16),
            jax.ShapeDtypeStruct((CPAD, C), BF16),
            jax.ShapeDtypeStruct((DP, 8, WIDE), BF16),
        ),
        in_specs=[anywhere, pl.BlockSpec(memory_space=pltpu.SMEM)] + [anywhere] * 5,
        out_specs=(vmem,) * 5,
        scratch_shapes=[
            pltpu.VMEM((MICRO, C, HEIGHT), BF16),
            pltpu.VMEM((MICRO, C, HEIGHT), BF16),
            rows_c,
            pltpu.VMEM((4, C, F), BF16),
            pltpu.VMEM((4, C, F), BF16),
            pltpu.VMEM((4, C, C), BF16),
            pltpu.VMEM((C, F), BF16),
            pltpu.VMEM((4, 8, F), F32),
            pltpu.VMEM((8, C), BF16),
            rows_c, rows_c, rows_c, rows_c,
            rows_c, rows_c,
            pltpu.VMEM((ROWS, C), F32),
            pltpu.VMEM((ROWS, 1), F32),
            pltpu.VMEM((ROWS, F), F32),
            pltpu.VMEM((ROWS, F), F32),
            rows_c, rows_c, rows_c,
            pltpu.VMEM((R, C), BF16),
            rows_c, rows_c, rows_c, rows_c, rows_c, rows_c,
            rows_f, rows_f,
            pltpu.VMEM((CPAD, C), F32),
        ]
        + item_scratch(C, WIDTHS[0])
        + item_scratch(C, WIDTHS[0])
        + item_scratch(C, WIDTHS[1])
        + item_scratch(C, WIDTHS[1])
        + item_scratch(CPAD // 2, C)
        + [dma((6,))]
        + [dma((N,))] * 8
        + [dma((5, N))] * 2
        + [dma((N,))] * 2
        + [dma((3, 12))] * 2
        + [dma((3,))] * 2
        + item_sems() * 5
        + [dma((DP - 1,))] * 2,
        compiler_params=pltpu.CompilerParams(
            collective_id=0, has_side_effects=True, vmem_limit_bytes=60 * 1024 * 1024
        ),
        name="relay",
    )(
        jnp.swapaxes(latents, 1, 2), steps, jnp.swapaxes(cotangent, 1, 2),
        w_in[0], jnp.swapaxes(w_out[0], 0, 1), w_time[0], w_skip[0],
    )
    wide = pl.BlockSpec((BLOCK, F), lambda i: (i, 0))
    narrow = pl.BlockSpec((BLOCK, C), lambda i: (i, 0))
    turned_rows = pl.BlockSpec((MICRO, BLOCK, HEIGHT), lambda i: (0, i, 0))
    grad_out_t, grad_in, grad_time, grad_skip, out_t = pl.pallas_call(
        finishing,
        grid=(C // BLOCK,),
        out_shape=(
            jax.ShapeDtypeStruct((C, F), F32),
            jax.ShapeDtypeStruct((C, F), F32),
            jax.ShapeDtypeStruct((C, F), F32),
            jax.ShapeDtypeStruct((C, C), F32),
            jax.ShapeDtypeStruct((MICRO, C, HEIGHT), BF16),
        ),
        in_specs=[wide, wide, narrow, pl.BlockSpec((DP * 8, WIDE), lambda i: (0, 0)), turned_rows],
        out_specs=(wide, wide, wide, narrow, turned_rows),
        scratch_shapes=[pltpu.VMEM((C, DP * 8), BF16)],
        name="finishing",
    )(ga, gb, gc, trow.reshape(DP * 8, WIDE), out_t)
    return (
        jnp.swapaxes(out_t, 1, 2)[None],
        grad_in[None], jnp.swapaxes(grad_out_t, 0, 1)[None], grad_time[None], grad_skip[None],
    )


def solution(mesh):
    placed = (
        P(None, "dp", None),
        P("dp", None),
        P(None, "dp", None),
        P("section", None, None),
        P("section", None, None),
        P("section", None, None),
        P("section", None, None),
    )
    return jax.shard_map(
        local,
        mesh=mesh,
        in_specs=placed,
        out_specs=(
            P("section", None, "dp", None),
            P("section", None, None),
            P("section", None, None),
            P("section", None, None),
            P("section", None, None),
        ),
        check_vma=False,
    )
```
